128 devices in a mesh: sp: 32 (over x, z_hi, y), ch: 4 (over z_lo, core).
Axes of the slice: x: 4, y: 4, z: 4 (z_hi: 2, z_lo: 2; z = z_hi * 2 + z_lo), core: 2. Of those that a mesh axis runs over, the one named last changes fastest.
Arguments:
- x_in: bfloat16 [256, 64, 128], P('ch', 'sp'), may hold values from -6 to 6
- gate_in: bfloat16 [256, 64, 128], P('ch', 'sp'), may hold values from -6 to 6
- conv_weight: float32 [256, 9], P('ch'), may hold values from -2 to 2
- conv_bias: float32 [256], P('ch'), may hold values from -0.5 to 0.5
- proj_weight: bfloat16 [4, 40, 256], P(None, None, 'ch'), may hold values from -0.375 to 0.375
- dt_weight: float32 [4, 256, 8], P(None, 'ch'), may hold values from -2 to 2
- dt_bias: float32 [4, 256], P(None, 'ch'), may hold values from -2 to 1
- decay_rate: float32 [4, 256, 16], P(None, 'ch'), may hold values from 0.0005 to 0.1
- skip_gain: float32 [4, 256], P(None, 'ch'), may hold values from 0.5 to 1.5
- norm_gain: float32 [256], P('ch'), may hold values from 0.5 to 1.5
- norm_bias: float32 [256], P('ch'), may hold values from -0.5 to 0.5
Outputs:
- mixed: bfloat16 [256, 64, 128], P('ch', 'sp')
The draws below stay inside these ranges and needn't reach their ends.
All inputs are finite; a program needn't handle non-finite values.
Results may differ from the reference program's by a relative error of at most 0.014.
Values may be sent and summed in bfloat16 or wider, within the bound.
No kernel may reach another device: no remote copies, remote signals or barrier semaphores. Data moves between devices by JAX's collectives and lax.ppermute only.
A program may use at most 64 MiB of HBM per device.

```python
import math
import jax
import jax.numpy as jnp
from jax import lax

C = 256
N = 16
R = 8
H = 64
W = 128
N_CH = 4


def block_levels(key, shape, pieces, low, top_value):
    def one(axis_at, shards_of):
        steps = jax.random.uniform(jax.random.fold_in(jax.random.fold_in(key, 6), axis_at), (shards_of,), jnp.float32, low / len(pieces), top_value / len(pieces))
        return jnp.repeat(jnp.exp(steps), shape[axis_at] // shards_of).reshape((-1,) + (1,) * (len(shape) - axis_at - 1))

    level = one(*pieces[0])
    for cut in pieces[1:]:
        level = level * one(*cut)
    return level


def scatter_about(rng, shape, deviation, reach, pieces=(), dtype=jnp.bfloat16):
    entries = deviation * jax.random.normal(rng, shape, jnp.float32)
    if pieces:
        entries = entries * block_levels(rng, shape, pieces, -0.22, 0.18)
    return jnp.clip(entries, -reach, reach).astype(dtype)


def setup_inputs(seed: int = 0) -> dict:
    key_of = jax.random.split(jax.random.key(seed), 12)
    x_in = scatter_about(key_of[0], (C, H, W), 1.0, 6.0, ((0, 4), (1, 32)))
    gate_in = scatter_about(key_of[1], (C, H, W), 1.0, 6.0, ((0, 4), (1, 32)))
    conv_weight = scatter_about(key_of[2], (C, 9), 9 ** -0.5, 2.0, ((0, 4),), jnp.float32)
    conv_bias = jnp.clip(jax.random.uniform(key_of[3], (C,), jnp.float32, -0.5, 0.5) * block_levels(key_of[3], (C,), ((0, 4),), -0.4, 0.0), -0.5, 0.5)
    proj_weight = scatter_about(key_of[4], (4, R + 2 * N, C), C ** -0.5, 0.375, ((2, 4),))
    dt_weight = scatter_about(key_of[5], (4, C, R), R ** -0.5, 2.0, ((1, 4),), jnp.float32)
    dt_bias = jnp.clip(-2.0 + 3.0 * jax.random.uniform(key_of[6], (4, C), jnp.float32) ** block_levels(key_of[6], (4, C), ((1, 4),), -0.2, 0.2), -2.0, 1.0)
    decay_rate = jnp.clip(jnp.exp(math.log(0.1) - 5.2983173 * jax.random.uniform(key_of[7], (4, C, N), jnp.float32) ** block_levels(key_of[7], (4, C, N), ((1, 4),), -0.2, 0.2)), 0.0005, 0.1)
    skip_gain = jnp.clip(0.5 + 1.0 * jax.random.uniform(key_of[8], (4, C), jnp.float32) ** block_levels(key_of[8], (4, C), ((1, 4),), -0.2, 0.2), 0.5, 1.5)
    norm_gain = jnp.clip(1.0 + 0.1 * jax.random.normal(key_of[9], (C,), jnp.float32), 0.5, 1.5)
    norm_bias = jnp.clip(jax.random.uniform(key_of[10], (C,), jnp.float32, -0.5, 0.5) * block_levels(key_of[10], (C,), ((0, 4),), -0.4, 0.0), -0.5, 0.5)
    return {"x_in": x_in, "gate_in": gate_in, "conv_weight": conv_weight, "conv_bias": conv_bias, "proj_weight": proj_weight, "dt_weight": dt_weight, "dt_bias": dt_bias, "decay_rate": decay_rate, "skip_gain": skip_gain, "norm_gain": norm_gain, "norm_bias": norm_bias}


def conv_silu(padded, conv_weight, conv_bias, rows, cols):
    total = jnp.zeros((padded.shape[0], rows, cols), jnp.float32) + conv_bias[:, None, None]
    for offset in range(9):
        down_shift = offset // 3
        side_shift = offset % 3
        window = padded[:, down_shift:down_shift + rows, side_shift:side_shift + cols].astype(jnp.float32)
        total = total + conv_weight[:, offset][:, None, None] * window
    return jax.nn.silu(total).astype(jnp.bfloat16)

def time_steps(low_rank, dt_weight, dt_bias):
    total = jnp.zeros(low_rank.shape[1:], jnp.float32)[None] + dt_bias[:, None, None]
    for rank_index in range(low_rank.shape[0]):
        total = total + dt_weight[:, rank_index][:, None, None] * low_rank[rank_index].astype(jnp.float32)[None]
    return jax.nn.softplus(total)

def line_scan(inputs, deltas, b_coef, c_coef, rates, skip_gain, reverse):
    moved = tuple((jnp.moveaxis(array, -1, 0) for array in (inputs, deltas, b_coef, c_coef)))

    def advance(states, items):
        values_now, delta_now, b_now, c_now = items
        decays = jnp.exp(-delta_now[:, None, :] * rates[:, :, None])
        states = decays * states + (delta_now * values_now)[:, None, :] * b_now[None, :, :]
        output = lax.optimization_barrier(jnp.sum(c_now[None, :, :] * states, axis=1)) + skip_gain[:, None] * values_now
        return (states, output)
    initial = jnp.zeros((inputs.shape[0], rates.shape[1], inputs.shape[1]), jnp.float32)
    _, outputs = lax.scan(advance, initial, moved, reverse=reverse)
    return jnp.moveaxis(outputs, 0, -1)

def projections(conv_out, proj_rows):
    chans, rows, cols = conv_out.shape
    group_size = chans // N_CH
    flattened = conv_out.reshape(chans, rows * cols)
    total = jnp.zeros((proj_rows.shape[0], rows * cols), jnp.float32)
    for group_index in range(N_CH):
        lower = group_index * group_size
        partial_sum = jnp.dot(proj_rows[:, lower:lower + group_size], flattened[lower:lower + group_size], preferred_element_type=jnp.float32)
        rounded = lax.optimization_barrier(partial_sum.astype(jnp.bfloat16))
        total = total + rounded.astype(jnp.float32)
    return total.astype(jnp.bfloat16).reshape(proj_rows.shape[0], rows, cols)

def reference(x_in, gate_in, conv_weight, conv_bias, proj_weight, dt_weight, dt_bias, decay_rate, skip_gain, norm_gain, norm_bias):
    chans, rows, cols = x_in.shape
    rank = dt_weight.shape[2]
    states = decay_rate.shape[2]
    width_proj = rank + 2 * states
    padded = jnp.pad(x_in, ((0, 0), (1, 1), (1, 1)))
    conv_out = conv_silu(padded, conv_weight, conv_bias, rows, cols)
    proj_all = projections(conv_out, proj_weight.reshape(4 * width_proj, chans)).reshape(4, width_proj, rows, cols)
    values = conv_out.astype(jnp.float32)
    horizontal = jnp.zeros((chans, rows, cols), jnp.float32)
    for direction in range(2):
        block = proj_all[direction]
        deltas = time_steps(block[:rank], dt_weight[direction], dt_bias[direction])
        horizontal = horizontal + line_scan(values, deltas, block[rank:rank + states].astype(jnp.float32), block[rank + states:].astype(jnp.float32), decay_rate[direction], skip_gain[direction], direction == 1)
    values_turned = values.transpose(0, 2, 1)
    vertical = jnp.zeros((chans, cols, rows), jnp.float32)
    for direction in range(2, 4):
        block = proj_all[direction].transpose(0, 2, 1)
        deltas = time_steps(block[:rank], dt_weight[direction], dt_bias[direction])
        vertical = vertical + line_scan(values_turned, deltas, block[rank:rank + states].astype(jnp.float32), block[rank + states:].astype(jnp.float32), decay_rate[direction], skip_gain[direction], direction == 3)
    vertical = lax.optimization_barrier(vertical.transpose(0, 2, 1).astype(jnp.bfloat16))
    combined = horizontal + vertical.astype(jnp.float32)
    mean = lax.optimization_barrier(jnp.sum(combined, axis=0)) / chans
    var = lax.optimization_barrier(jnp.sum(combined * combined, axis=0)) / chans - mean * mean
    normed = (combined - mean[None]) * lax.rsqrt(var[None] + 1e-05) * norm_gain[:, None, None] + norm_bias[:, None, None]
    return (normed * jax.nn.silu(gate_in.astype(jnp.float32))).astype(jnp.bfloat16)
```

```python
import math

import jax
import jax.numpy as jnp
from jax import lax
from jax.experimental import pallas as pl
from jax.experimental.pallas import tpu as pltpu
from jax.sharding import PartitionSpec as P

F32 = jnp.float32
BF16 = jnp.bfloat16
LANES = 128
EXACT = lax.Precision.HIGHEST
NEG_LOG2E = -1.0 / math.log(2.0)

PROJ_ROWS = 160
VEC_ROWS = 64
WBUF_ROWS = PROJ_ROWS + 2 * VEC_ROWS


def iota(shape, axis):
    return lax.broadcasted_iota(jnp.int32, shape, axis)


def dup_matrix(chans):
    return jnp.where(iota((chans, 2 * chans), 1) // 2 == iota((chans, 2 * chans), 0), 1.0, 0.0).astype(F32)


def dup_rows(value, dup):
    return jnp.dot(value, dup, preferred_element_type=F32, precision=EXACT)


def dup_cols(value, dup):
    return lax.dot_general(
        value, dup, (((0,), (0,)), ((), ())), preferred_element_type=F32, precision=EXACT
    )


def softplus(x):
    return jnp.maximum(x, 0.0) + jnp.log1p(jnp.exp(-jnp.abs(x)))


def silu(x):
    return x * jax.nn.sigmoid(x)


def roll(x, shift, axis):
    return pltpu.roll(x, shift % x.shape[axis], axis)


def prep_kernel(x_ref, cw_ref, cb_ref, pw_ref, dtw_ref, dtb_ref, rate_ref, skip_ref, send_ref, w_ref, scr, vec):
    turned = x_ref[...].astype(F32).T
    scr[pl.ds(12, LANES, stride=4), :] = turned
    scr[pl.ds(9, LANES, stride=4), :] = turned
    scr[pl.ds(6, LANES, stride=4), :] = turned
    scr[pl.ds(11, LANES, stride=4), :] = jnp.zeros((LANES, LANES), F32)
    scr[8:9, :] = jnp.zeros((1, LANES), F32)
    scr[8 + 4 * 127 + 2 : 8 + 4 * 127 + 3, :] = jnp.zeros((1, LANES), F32)
    send_ref[...] = scr[8 : 8 + 4 * LANES, :].astype(BF16)

    chans = cw_ref.shape[0]
    dup = dup_matrix(chans)
    dup_b = dup.astype(BF16)
    first = jnp.dot(
        jnp.concatenate([pw_ref[0].astype(F32), pw_ref[1].astype(F32)], axis=0).astype(BF16),
        dup_b,
        preferred_element_type=F32,
    )
    w_ref[0:80, :] = first.astype(BF16)
    third = pw_ref[2].astype(F32)
    fourth = pw_ref[3].astype(F32)
    rest = jnp.concatenate([third[0:8], fourth[0:8], third[8:40], fourth[8:40]], axis=0)
    w_ref[80:160, :] = jnp.dot(rest.astype(BF16), dup_b, preferred_element_type=F32).astype(BF16)

    vec[0:9, :] = dup_cols(cw_ref[...], dup)
    vec[9:10, :] = dup_rows(cb_ref[...], dup)
    vec[10:12, :] = dup_rows(dtb_ref[...], dup)[2:4]
    vec[12:14, :] = dup_rows(skip_ref[...], dup)[2:4]
    vec[14:16, :] = jnp.zeros((2, LANES), F32)
    vec[16:24, :] = dup_cols(dtw_ref[2], dup)
    vec[24:32, :] = dup_cols(dtw_ref[3], dup)
    vec[32:48, :] = dup_cols(rate_ref[2], dup)
    vec[48:64, :] = dup_cols(rate_ref[3], dup)
    whole = vec[...]
    high = whole.astype(BF16)
    w_ref[PROJ_ROWS : PROJ_ROWS + VEC_ROWS, :] = high
    w_ref[PROJ_ROWS + VEC_ROWS :, :] = (whole - high.astype(F32)).astype(BF16)


def scan_pair(steps, rates, delta_refs, drive_refs, b_at, c_at, y_refs, row_of):
    width = rates[0].shape[1]
    states = [jnp.zeros(rates[0].shape, F32) for _ in range(2)]
    for step in range(steps):
        for way in range(2):
            at = step if way == 0 else steps - 1 - step
            row = row_of(at)
            delta = delta_refs[way][row : row + 1, :]
            drive = drive_refs[way][row : row + 1, :]
            decay = jnp.exp2(delta * rates[way])
            states[way] = decay * states[way] + drive * b_at(way, at, width)
            y_refs[way][row : row + 1, :] = jnp.sum(
                c_at(way, at, width) * states[way], axis=0, keepdims=True
            )


def column_kernel(recv_ref, own_ref, w1_ref, w2_ref, w3_ref, send_ref, scr, wall, delta2, delta3, drive2, drive3, y2, y3):
    me = lax.axis_index("ch")
    slabs = LANES // 4
    wall[me] = own_ref[...]
    wall[me ^ 1] = w1_ref[...]
    wall[me ^ 2] = w2_ref[...]
    wall[me ^ 3] = w3_ref[...]

    scr[0:16, :] = jnp.zeros((16, LANES), F32)
    scr[16 + 512 : 32 + 512, :] = jnp.zeros((16, LANES), F32)
    scr[16 : 16 + 512, :] = recv_ref[...].astype(F32)

    even = iota((slabs, LANES), 1) % 2 == 0
    vecs = []
    conv = []
    for group in range(4):
        vec = wall[group, PROJ_ROWS : PROJ_ROWS + VEC_ROWS, :].astype(F32) + wall[
            group, PROJ_ROWS + VEC_ROWS :, :
        ].astype(F32)
        vecs.append(vec)
        total = jnp.zeros((slabs, LANES), F32) + vec[9:10, :]
        for side in range(3):
            base = 16 + 4 * group + side
            above = scr[pl.ds(base - 16, slabs, stride=16), :]
            here = scr[pl.ds(base, slabs, stride=16), :]
            below = scr[pl.ds(base + 16, slabs, stride=16), :]
            here_next = roll(here, -1, 1)
            here_prev = roll(here, 1, 1)
            up = jnp.where(even, roll(above, -1, 1), here_prev)
            down = jnp.where(even, here_next, roll(below, 1, 1))
            total = total + vec[side : side + 1, :] * up
            total = total + vec[3 + side : 4 + side, :] * here
            total = total + vec[6 + side : 7 + side, :] * down
        conv.append(silu(total).astype(BF16).astype(F32))

    evens = [jnp.where(even, conv[2 * p], roll(conv[2 * p + 1], 1, 1)) for p in range(2)]
    odds = [jnp.where(even, roll(conv[2 * p], -1, 1), conv[2 * p + 1]) for p in range(2)]
    values = jnp.concatenate(
        [jnp.concatenate(evens, axis=1), jnp.concatenate(odds, axis=1)], axis=0
    )
    values_b = values.astype(BF16)

    even_w = iota((WBUF_ROWS, LANES), 1) % 2 == 0
    weights = jnp.concatenate(
        [
            jnp.where(even_w, wall[2 * p].astype(F32), wall[2 * p + 1].astype(F32))
            for p in range(2)
        ],
        axis=1,
    )
    proj_w = weights[0:PROJ_ROWS].astype(BF16)
    vec = weights[PROJ_ROWS : PROJ_ROWS + VEC_ROWS] + weights[PROJ_ROWS + VEC_ROWS :]

    nt = (((1,), (1,)), ((), ()))
    proj = lax.dot_general(values_b, proj_w[0:128], nt, preferred_element_type=F32)
    proj = proj.astype(BF16).astype(F32)
    turned = lax.dot_general(proj_w[96:160], values_b, nt, preferred_element_type=F32)
    turned = turned.astype(BF16).astype(F32)

    low = lax.dot_general(values_b, proj_w[80:96], nt, preferred_element_type=F32)
    low = low.astype(BF16).astype(F32)
    dt_rows = vec[16:32]
    second_half = iota((16, 256), 0) >= 8
    for way, (delta_ref, drive_ref) in enumerate(((delta2, drive2), (delta3, drive3))):
        chosen = jnp.where(second_half == (way == 1), dt_rows, 0.0)
        delta = softplus(
            jnp.dot(low, chosen, preferred_element_type=F32, precision=EXACT)
            + vec[10 + way : 11 + way, :]
        )
        delta_ref[...] = delta
        drive_ref[...] = delta * values
    rates = [vec[32 + 16 * way : 48 + 16 * way] * NEG_LOG2E for way in range(2)]

    def row_of(at):
        return (at % 2) * slabs + at // 2

    def part(way, at, width, offset):
        column = row_of(at)
        first = 32 * way + offset
        return jnp.broadcast_to(turned[first : first + 16, column : column + 1], (16, width))

    scan_pair(
        2 * slabs,
        rates,
        (delta2, delta3),
        (drive2, drive3),
        lambda way, at, width: part(way, at, width, 0),
        lambda way, at, width: part(way, at, width, 16),
        (y2, y3),
        row_of,
    )

    y = y2[...] + y3[...] + (vec[12:13] + vec[13:14]) * values
    for group in range(4):
        pair = slice(LANES * (group // 2), LANES * (group // 2) + LANES)
        y_even = y[0:slabs, pair]
        y_odd = y[slabs:, pair]
        if group % 2 == 0:
            back = jnp.where(even, y_even, roll(y_odd, 1, 1))
        else:
            back = jnp.where(even, roll(y_even, -1, 1), y_odd)
        base = 4 * group
        scr[pl.ds(base, slabs, stride=16), :] = back
        scr[pl.ds(base + 1, slabs, stride=16), :] = conv[group]
        scr[pl.ds(base + 2, slabs, stride=16), :] = proj[0:slabs]
        scr[pl.ds(base + 3, slabs, stride=16), :] = proj[slabs:]
    send_ref[...] = scr[0:512, :].astype(BF16)


def row_kernel(recv_ref, dtw_ref, dtb_ref, rate_ref, skip_ref, comb_ref, sums_ref, scr, delta0, delta1, drive0, drive1, y0, y1):
    scr[...] = recv_ref[...].astype(F32)
    cols = LANES
    vertical = scr[pl.ds(0, cols, stride=4), :]
    values = scr[pl.ds(1, cols, stride=4), :]
    proj = [scr[pl.ds(2 + row, cols, stride=4), :] for row in range(2)]

    chans = dtw_ref.shape[1]
    dup = dup_matrix(chans)
    bias = dup_rows(dtb_ref[...], dup)
    skip = dup_rows(skip_ref[...], dup)
    lane_row = iota((8, LANES), 1) % 2
    rates = []
    for way, (delta_ref, drive_ref) in enumerate(((delta0, drive0), (delta1, drive1))):
        dt_rows = dup_cols(dtw_ref[way], dup)
        total = jnp.zeros((cols, LANES), F32) + bias[way : way + 1, :]
        for row in range(2):
            mine = jnp.where(lane_row == row, dt_rows, 0.0)
            parts = [mine, jnp.zeros((LANES - 40 * way - 8, LANES), F32)]
            if way:
                parts = [jnp.zeros((40 * way, LANES), F32)] + parts
            total = total + jnp.dot(
                proj[row], jnp.concatenate(parts, axis=0), preferred_element_type=F32, precision=EXACT
            )
        delta = softplus(total)
        delta_ref[...] = delta
        drive_ref[...] = delta * values
        rates.append(dup_cols(rate_ref[way], dup) * NEG_LOG2E)

    turned = [p.T for p in proj]
    even = iota((16, LANES), 1) % 2 == 0

    def part(way, at, width, offset):
        first = 40 * way + offset
        left = jnp.broadcast_to(turned[0][first : first + 16, at : at + 1], (16, width))
        right = jnp.broadcast_to(turned[1][first : first + 16, at : at + 1], (16, width))
        return jnp.where(even, left, right)

    scan_pair(
        cols,
        rates,
        (delta0, delta1),
        (drive0, drive1),
        lambda way, at, width: part(way, at, width, 8),
        lambda way, at, width: part(way, at, width, 24),
        (y0, y1),
        lambda at: at,
    )
    combined = y0[...] + y1[...] + (skip[0:1] + skip[1:2]) * values + vertical
    turned_back = combined.T
    comb_ref[...] = turned_back
    for index, value in enumerate((turned_back, turned_back * turned_back)):
        part_sum = value[0:8]
        for tile in range(1, LANES // 8):
            part_sum = part_sum + value[8 * tile : 8 * tile + 8]
        part_sum = part_sum + roll(part_sum, 4, 0)
        part_sum = part_sum + roll(part_sum, 2, 0)
        sums_ref[8 * index : 8 * index + 8, :] = part_sum


def norm_kernel(total_chans, comb_ref, s0_ref, s1_ref, s2_ref, s3_ref, gate_ref, gain_ref, bias_ref, out_ref):
    sums = (s0_ref[...] + s1_ref[...]) + (s2_ref[...] + s3_ref[...])
    mean = sums[0:8] / total_chans
    var = sums[8:16] / total_chans - mean * mean
    scale = lax.rsqrt(var + 1e-05)
    chans = gain_ref.shape[1]
    pick = iota((LANES, chans), 0) // 2 == iota((LANES, chans), 1)
    gain = jnp.sum(jnp.where(pick, gain_ref[...], 0.0), axis=1, keepdims=True)
    bias = jnp.sum(jnp.where(pick, bias_ref[...], 0.0), axis=1, keepdims=True)
    gate = silu(gate_ref[...].astype(F32))
    comb = comb_ref[...]
    means = jnp.concatenate([mean] * (LANES // 8), axis=0)
    scales = jnp.concatenate([scale] * (LANES // 8), axis=0)
    normed = (comb - means) * scales * gain + bias
    out_ref[...] = (normed * gate).astype(BF16)


VMEM = pl.BlockSpec(memory_space=pltpu.VMEM)


def call(kernel, name, outs, scratch, inputs):
    single = not isinstance(outs, (list, tuple))
    return pl.pallas_call(
        kernel,
        out_shape=outs,
        in_specs=[VMEM] * len(inputs),
        out_specs=VMEM if single else [VMEM] * len(outs),
        scratch_shapes=scratch,
        name=name,
        compiler_params=pltpu.CompilerParams(vmem_limit_bytes=24 << 20),
    )(*inputs)


def others(value):
    return [
        lax.ppermute(value, "ch", [(i, i ^ k) for i in range(lax.axis_size("ch"))])
        for k in (1, 2, 3)
    ]


def exchange(value):
    return lax.all_to_all(value, ("sp", "ch"), split_axis=0, concat_axis=0, tiled=True)


def on_device(
    x_in,
    gate_in,
    conv_weight,
    conv_bias,
    proj_weight,
    dt_weight,
    dt_bias,
    decay_rate,
    skip_gain,
    norm_gain,
    norm_bias,
):
    chans, rows, cols = x_in.shape
    total_chans = chans * lax.axis_size("ch")
    flat = (chans * rows, cols)
    struct = jax.ShapeDtypeStruct
    buffer = struct((4 * cols, LANES), BF16)

    def vm(*shape):
        return pltpu.VMEM(shape, F32)

    send, weights = call(
        prep_kernel,
        "prep",
        [buffer, struct((WBUF_ROWS, LANES), BF16)],
        [vm(4 * cols + 16, LANES), vm(VEC_ROWS, LANES)],
        [
            x_in.reshape(flat),
            conv_weight,
            conv_bias.reshape(1, chans),
            proj_weight,
            dt_weight,
            dt_bias,
            decay_rate,
            skip_gain,
        ],
    )
    shared = others(weights)
    received = exchange(send)
    send = call(
        column_kernel,
        "columns",
        buffer,
        [vm(4 * cols + 32, LANES), pltpu.VMEM((4, WBUF_ROWS, LANES), BF16)] + [vm(64, 256)] * 6,
        [received, weights] + shared,
    )
    received = exchange(send)
    combined, sums = call(
        row_kernel,
        "rows",
        [struct((LANES, cols), F32), struct((16, cols), F32)],
        [vm(4 * cols, LANES)] + [vm(cols, LANES)] * 6,
        [received, dt_weight, dt_bias, decay_rate, skip_gain],
    )
    out = call(
        lambda *refs: norm_kernel(total_chans, *refs),
        "norm",
        struct(flat, BF16),
        [],
        [combined, sums]
        + others(sums)
        + [gate_in.reshape(flat), norm_gain.reshape(1, chans), norm_bias.reshape(1, chans)],
    )
    return out.reshape(chans, rows, cols)


def solution(mesh):
    placed = (
        P("ch", "sp", None),
        P("ch", "sp", None),
        P("ch", None),
        P("ch"),
        P(None, None, "ch"),
        P(None, "ch", None),
        P(None, "ch"),
        P(None, "ch", None),
        P(None, "ch"),
        P("ch"),
        P("ch"),
    )
    return jax.shard_map(
        on_device, mesh=mesh, in_specs=placed, out_specs=P("ch", "sp", None), check_vma=False
    )
```

```python
import math

import jax
import jax.numpy as jnp
from jax import lax
from jax.experimental import pallas as pl
from jax.experimental.pallas import tpu as pltpu
from jax.sharding import PartitionSpec as P

F32 = jnp.float32
BF16 = jnp.bfloat16
LANES = 128
EXACT = lax.Precision.HIGHEST
NEG_LOG2E = -1.0 / math.log(2.0)

CHUNK = 8
X_ROWS = 3
PROJ_PAIRS = 80
VEC_PAIRS = 32


def iota(shape, axis):
    return lax.broadcasted_iota(jnp.int32, shape, axis)


def spread(chans, offset):
    lane = iota((chans, 2 * chans), 1)
    return jnp.where(lane == 2 * iota((chans, 2 * chans), 0) + offset, 1.0, 0.0).astype(F32)


def dup_rows(value, dup):
    return jnp.dot(value, dup, preferred_element_type=F32, precision=EXACT)


def softplus(x):
    return jnp.maximum(x, 0.0) + jnp.log1p(jnp.exp(-jnp.abs(x)))


def silu(x):
    return x * jax.nn.sigmoid(x)


def roll(x, shift, axis):
    return pltpu.roll(x, shift % x.shape[axis], axis)


def prep_kernel(*refs):
    count = 8
    sources, send_ref, scr, vec, packed = refs[:count], *refs[count : count + 4]
    loaded, arrived = refs[count + 4 : -1], refs[-1]
    copies = [
        pltpu.make_async_copy(source, target, arrived.at[index])
        for index, (source, target) in enumerate(zip(sources, loaded))
    ]
    for copy in copies:
        copy.start()
    for copy in copies:
        copy.wait()
    x_ref, cw_ref, cb_ref, pw_ref, dtw_ref, dtb_ref, rate_ref, skip_ref = loaded
    chans = cw_ref.shape[1]
    even, odd = spread(chans, 0), spread(chans, 1)
    even_b, odd_b = even.astype(BF16), odd.astype(BF16)
    half = VEC_PAIRS
    vec[0:9, :] = cw_ref[...]
    vec[9:10, :] = cb_ref[...]
    vec[10:12, :] = dtb_ref[2:4, :]
    vec[12:14, :] = skip_ref[2:4, :]
    vec[14:16, :] = jnp.zeros((2, chans), F32)
    vec[16:24, :] = dtw_ref[2]
    vec[24:32, :] = dtw_ref[3]
    vec[32:48, :] = rate_ref[2]
    vec[48:64, :] = rate_ref[3]
    whole = vec[...]
    high = whole.astype(BF16)
    low = (whole - high.astype(F32)).astype(BF16)

    def pack(first, second):
        return jnp.dot(first, even_b, preferred_element_type=F32) + jnp.dot(
            second, odd_b, preferred_element_type=F32
        )

    third = pw_ref[2].astype(F32)
    fourth = pw_ref[3].astype(F32)
    rest = jnp.concatenate([third[0:8], fourth[0:8], third[8:40], fourth[8:40]], axis=0)
    packed[0:40, :] = pack(pw_ref[0], rest[0:40].astype(BF16))
    packed[40:80, :] = pack(pw_ref[1], rest[40:80].astype(BF16))
    packed[80:112, :] = pack(high[0:half], high[half:])
    packed[112:144, :] = pack(low[0:half], low[half:])
    packed[144:160, :] = jnp.zeros((16, LANES), F32)

    turned = x_ref[...].astype(F32).T
    base = 2 * CHUNK
    scr[pl.ds(base + CHUNK, LANES, stride=CHUNK), :] = turned
    scr[pl.ds(base + 1, LANES, stride=CHUNK), :] = turned
    scr[pl.ds(base - CHUNK + 2, LANES, stride=CHUNK), :] = turned
    scr[base : base + 1, :] = jnp.zeros((1, LANES), F32)
    last = base + CHUNK * (LANES - 1) + 2
    scr[last : last + 1, :] = jnp.zeros((1, LANES), F32)
    slab = lax.axis_index("sp")
    for piece in range(CHUNK - X_ROWS):
        row = packed[pl.ds(32 * piece + slab, 1), :]
        scr[pl.ds(base + X_ROWS + piece, LANES, stride=CHUNK), :] = jnp.broadcast_to(row, (LANES, LANES))
    send_ref[...] = scr[base : base + CHUNK * LANES, :].astype(BF16)


def scan_pair(steps, rates, delta_ref, drive_ref, b_at, c_at, part_ref, row_of):
    blocks = delta_ref.shape[1]
    shape = (16, LANES)
    states = [[jnp.zeros(shape, F32) for _ in range(blocks)] for _ in range(2)]
    for step in range(steps):
        for way in range(2):
            at = step if way == 0 else steps - 1 - step
            row = row_of(at)
            b_now, c_now = b_at(way, at), c_at(way, at)
            for block in range(blocks):
                delta = delta_ref[way, block, row : row + 1, :]
                drive = drive_ref[way, block, row : row + 1, :]
                decay = jnp.exp2(delta * rates[way][block])
                state = decay * states[way][block] + drive * b_now
                states[way][block] = state
                product = c_now * state
                part_ref[way, block, 8 * row : 8 * row + 8, :] = product[0:8] + product[8:16]


def outputs_of(part_ref, block, half_ref):
    rows = part_ref.shape[2] // 8
    total = None
    for way in range(2):
        for lane_row in range(4):
            term = part_ref[way, block, pl.ds(lane_row, 2 * rows, stride=4), :]
            total = term if total is None else total + term
    half_ref[0 : 2 * rows, :] = total
    return half_ref[pl.ds(0, rows, stride=2), :] + half_ref[pl.ds(1, rows, stride=2), :]


def halves(value):
    high = value.astype(BF16)
    return high, (value - high.astype(F32)).astype(BF16)


def two_part_dot(value, high, low):
    return jnp.dot(value, high, preferred_element_type=F32) + jnp.dot(
        value, low, preferred_element_type=F32
    )


def column_kernel(recv_ref, send_ref, flat_scr, scr, delta_scr, drive_scr, part_scr, half_scr, turned_scr):
    slabs = LANES // 4
    pad = 8
    flat_scr[...] = recv_ref[...].astype(F32)
    for row in range(CHUNK):
        scr[row, pad - 4 : pad, :] = jnp.zeros((4, LANES), F32)
        scr[row, pad + LANES : pad + LANES + 4, :] = jnp.zeros((4, LANES), F32)
        scr[row, pad : pad + LANES, :] = flat_scr[pl.ds(row, LANES, stride=CHUNK), :]

    even = iota((slabs, LANES), 1) % 2 == 0
    vecs = []
    projs = []
    conv = []
    for group in range(4):

        def rows_of(row, shift):
            return scr[row, pl.ds(pad + group + 4 * shift, slabs, stride=4), :]

        pieces = [rows_of(row, 0) for row in range(X_ROWS, CHUNK)]
        projs.append([pieces[0], pieces[1], pieces[2][0:16]])
        vec = jnp.concatenate([pieces[2][16:32], pieces[3][0:16]], axis=0) + jnp.concatenate(
            [pieces[3][16:32], pieces[4][0:16]], axis=0
        )
        vecs.append(vec)
        taps = jnp.where(even[0:16], vec[0:16], roll(vec[0:16], 1, 1))
        total = jnp.zeros((slabs, LANES), F32) + taps[9:10, :]
        for side in range(3):
            here = rows_of(side, 0)
            up = jnp.where(even, roll(rows_of(side, -1), -1, 1), roll(here, 1, 1))
            down = jnp.where(even, roll(here, -1, 1), roll(rows_of(side, 1), 1, 1))
            total = total + taps[side : side + 1, :] * up
            total = total + taps[3 + side : 4 + side, :] * here
            total = total + taps[6 + side : 7 + side, :] * down
        conv.append(silu(total).astype(BF16).astype(F32))

    def from_even(left, right):
        mask = iota(left.shape, 1) % 2 == 0
        return jnp.where(mask, left, roll(right, 1, 1))

    def from_odd(left, right):
        mask = iota(left.shape, 1) % 2 == 0
        return jnp.where(mask, roll(left, -1, 1), right)

    def all_groups(take, parts):
        return jnp.concatenate([take(parts[0], parts[1]), take(parts[2], parts[3])], axis=1)

    values = jnp.concatenate([all_groups(from_even, conv), all_groups(from_odd, conv)], axis=0)
    values_b = values.astype(BF16)
    proj_w = jnp.concatenate(
        [
            all_groups(take, [p[piece] for p in projs])
            for take in (from_even, from_odd)
            for piece in range(3)
        ],
        axis=0,
    ).astype(BF16)
    vec = jnp.concatenate([all_groups(from_even, vecs), all_groups(from_odd, vecs)], axis=0)

    nt = (((1,), (1,)), ((), ()))
    proj = lax.dot_general(values_b, proj_w[0:128], nt, preferred_element_type=F32)
    proj = proj.astype(BF16).astype(F32)
    turned = lax.dot_general(proj_w[96:160], values_b, nt, preferred_element_type=F32)
    turned = turned.astype(BF16).astype(F32)

    turned_scr[...] = turned
    low = lax.dot_general(values_b, proj_w[80:96], nt, preferred_element_type=F32).astype(BF16)
    dt_rows = vec[16:32]
    second_half = iota((16, 256), 0) >= 8
    rates = []
    for way in range(2):
        chosen = jnp.where(second_half == (way == 1), dt_rows, 0.0)
        delta = softplus(two_part_dot(low, *halves(chosen)) + vec[10 + way : 11 + way, :])
        drive = delta * values
        scaled = vec[32 + 16 * way : 48 + 16 * way] * NEG_LOG2E
        rates.append([scaled[:, 0:LANES], scaled[:, LANES:]])
        for block in range(2):
            lanes = slice(LANES * block, LANES * block + LANES)
            delta_scr[way, block] = delta[:, lanes]
            drive_scr[way, block] = drive[:, lanes]

    def row_of(at):
        return (at % 2) * slabs + at // 2

    def part(way, at, offset):
        column = row_of(at)
        first = 32 * way + offset
        return jnp.broadcast_to(turned_scr[first : first + 16, column : column + 1], (16, LANES))

    scan_pair(
        2 * slabs,
        rates,
        delta_scr,
        drive_scr,
        lambda way, at: part(way, at, 0),
        lambda way, at: part(way, at, 16),
        part_scr,
        row_of,
    )

    skip = vec[12:13] + vec[13:14]
    for block in range(2):
        lanes = slice(LANES * block, LANES * block + LANES)
        y = outputs_of(part_scr, block, half_scr) + skip[:, lanes] * values[:, lanes]
        y_even, y_odd = y[0:slabs], y[slabs:]
        backs = (
            jnp.where(even, y_even, roll(y_odd, 1, 1)),
            jnp.where(even, roll(y_even, -1, 1), y_odd),
        )
        for bit in range(2):
            group = 2 * block + bit
            parts = (backs[bit], conv[group], proj[0:slabs], proj[slabs:])
            for row in range(4):
                scr[row, pl.ds(group, slabs, stride=4), :] = parts[row]
    for row in range(4):
        flat_scr[pl.ds(row, LANES, stride=4), :] = scr[row, 0:LANES, :]
    send_ref[...] = flat_scr[0 : 4 * LANES, :].astype(BF16)


def side_kernel(
    dtw_ref,
    dtb_ref,
    rate_ref,
    skip_ref,
    gain_ref,
    bias_ref,
    gate_ref,
    vec_ref,
    high_ref,
    low_ref,
    gate_out_ref,
    affine_ref,
):
    chans = dtw_ref.shape[2]
    dup = spread(chans, 0) + spread(chans, 1)
    vec_ref[0:16, :] = dup_rows(rate_ref[0], dup) * NEG_LOG2E
    vec_ref[16:32, :] = dup_rows(rate_ref[1], dup) * NEG_LOG2E
    vec_ref[32:36, :] = dup_rows(dtb_ref[...], dup)
    skip = dup_rows(skip_ref[...], dup)
    vec_ref[36:37, :] = skip[0:1] + skip[1:2]
    vec_ref[37:40, :] = jnp.zeros((3, LANES), F32)
    lane_row = iota((8, LANES), 1) % 2
    columns = []
    for way in range(2):
        dt_rows = dup_rows(dtw_ref[way], dup)
        column = []
        for row in range(2):
            column += [jnp.zeros((40 * way, LANES), F32)] if way else []
            column.append(jnp.where(lane_row == row, dt_rows, 0.0))
            column.append(jnp.zeros((LANES - 40 * way - 8, LANES), F32))
        columns.append(jnp.concatenate(column, axis=0))
    high_ref[...], low_ref[...] = halves(jnp.concatenate(columns, axis=1))
    gate_out_ref[...] = silu(gate_ref[...].astype(F32))
    pick = iota((LANES, LANES), 0) == iota((LANES, LANES), 1)
    for index, ref in enumerate((gain_ref, bias_ref)):
        lanes = dup_rows(ref[...], dup)
        column = jnp.sum(jnp.where(pick, lanes, 0.0), axis=1, keepdims=True)
        affine_ref[index] = jnp.broadcast_to(column, (LANES, LANES))


def row_kernel(
    recv_ref,
    vec_ref,
    high_ref,
    low_ref,
    comb_ref,
    sums_ref,
    scr,
    mixed_scr,
    delta_scr,
    drive_scr,
    part_scr,
    half_scr,
    turned_scr,
):
    cols = LANES
    scr[...] = recv_ref[...].astype(F32)
    vertical = scr[pl.ds(0, cols, stride=4), :]
    values = scr[pl.ds(1, cols, stride=4), :]
    proj = [scr[pl.ds(2 + row, cols, stride=4), :] for row in range(2)]

    both = jnp.concatenate(proj, axis=1).astype(BF16)
    low_rank = two_part_dot(both, high_ref[...], low_ref[...])
    rates = []
    for way in range(2):
        lanes = slice(LANES * way, LANES * way + LANES)
        delta = softplus(low_rank[:, lanes] + vec_ref[32 + way : 33 + way, :])
        delta_scr[way, 0] = delta
        drive_scr[way, 0] = delta * values
        rates.append([vec_ref[16 * way : 16 * way + 16, :]])

    for row in range(2):
        mixed_scr[pl.ds(row, cols, stride=2), :] = proj[row]
    turned_scr[...] = mixed_scr[...].T
    parity = iota((16, LANES), 1) % 2

    def part(way, at, offset):
        first = 40 * way + offset
        start = LANES * (at // 64)
        return jnp.take_along_axis(
            turned_scr[first : first + 16, start : start + LANES],
            parity + 2 * (at % 64),
            axis=1,
            mode="promise_in_bounds",
        )

    scan_pair(
        cols,
        rates,
        delta_scr,
        drive_scr,
        lambda way, at: part(way, at, 8),
        lambda way, at: part(way, at, 24),
        part_scr,
        lambda at: at,
    )
    combined = outputs_of(part_scr, 0, half_scr) + vec_ref[36:37, :] * values + vertical
    turned_back = combined.T
    comb_ref[...] = turned_back
    for index, value in enumerate((turned_back, turned_back * turned_back)):
        part_sum = value[0:8]
        for tile in range(1, LANES // 8):
            part_sum = part_sum + value[8 * tile : 8 * tile + 8]
        part_sum = part_sum + roll(part_sum, 4, 0)
        part_sum = part_sum + roll(part_sum, 2, 0)
        sums_ref[8 * index : 8 * index + 8, :] = part_sum


def norm_kernel(total_chans, comb_ref, s0_ref, s1_ref, s2_ref, s3_ref, gate_ref, affine_ref, out_ref):
    sums = (s0_ref[...] + s1_ref[...]) + (s2_ref[...] + s3_ref[...])
    mean = sums[0:8] / total_chans
    var = sums[8:16] / total_chans - mean * mean
    scale = lax.rsqrt(var + 1e-05)
    comb = comb_ref[...]
    means = jnp.concatenate([mean] * (LANES // 8), axis=0)
    scales = jnp.concatenate([scale] * (LANES // 8), axis=0)
    normed = (comb - means) * scales * affine_ref[0] + affine_ref[1]
    out_ref[...] = (normed * gate_ref[...]).astype(BF16)


VMEM = pl.BlockSpec(memory_space=pltpu.VMEM)


def call(kernel, name, outs, scratch, inputs, place=VMEM, grant=24 << 20):
    single = not isinstance(outs, (list, tuple))
    return pl.pallas_call(
        kernel,
        out_shape=outs,
        in_specs=[place] * len(inputs),
        out_specs=VMEM if single else [VMEM] * len(outs),
        scratch_shapes=scratch,
        name=name,
        compiler_params=pltpu.CompilerParams(vmem_limit_bytes=grant),
    )(*inputs)


def others(value):
    return [
        lax.ppermute(value, "ch", [(i, i ^ k) for i in range(lax.axis_size("ch"))])
        for k in (1, 2, 3)
    ]


def exchange(value):
    return lax.all_to_all(value, ("sp", "ch"), split_axis=0, concat_axis=0, tiled=True)


def on_device(
    x_in,
    gate_in,
    conv_weight,
    conv_bias,
    proj_weight,
    dt_weight,
    dt_bias,
    decay_rate,
    skip_gain,
    norm_gain,
    norm_bias,
):
    chans, rows, cols = x_in.shape
    total_chans = chans * lax.axis_size("ch")
    flat = (chans * rows, cols)
    struct = jax.ShapeDtypeStruct

    def vm(*shape):
        return pltpu.VMEM(shape, F32)

    dt_weight = dt_weight.transpose(0, 2, 1)
    decay_rate = decay_rate.transpose(0, 2, 1)
    arguments = [
        x_in.reshape(flat),
        conv_weight.T,
        conv_bias.reshape(1, chans),
        proj_weight,
        dt_weight,
        dt_bias,
        decay_rate,
        skip_gain,
    ]
    send = call(
        prep_kernel,
        "prep",
        struct((CHUNK * cols, LANES), BF16),
        [vm(CHUNK * (cols + 4), LANES), vm(2 * VEC_PAIRS, chans), vm(160, LANES)]
        + [pltpu.VMEM(value.shape, value.dtype) for value in arguments]
        + [pltpu.SemaphoreType.DMA((len(arguments),))],
        [pltpu.with_memory_space_constraint(value, pltpu.HBM) for value in arguments],
        pl.BlockSpec(memory_space=pltpu.HBM),
    )
    vec, high, low, gate, affine = call(
        side_kernel,
        "side",
        [
            struct((40, LANES), F32),
            struct((2 * LANES, 2 * LANES), BF16),
            struct((2 * LANES, 2 * LANES), BF16),
            struct((LANES, cols), F32),
            struct((2, LANES, cols), F32),
        ],
        [],
        [
            dt_weight,
            dt_bias,
            decay_rate,
            skip_gain,
            norm_gain.reshape(1, chans),
            norm_bias.reshape(1, chans),
            gate_in.reshape(flat),
        ],
    )
    send = call(
        column_kernel,
        "columns",
        struct((4 * cols, LANES), BF16),
        [
            vm(CHUNK * cols, LANES),
            vm(CHUNK, cols + 16, LANES),
            vm(2, 2, 64, LANES),
            vm(2, 2, 64, LANES),
            vm(2, 2, 8 * 64, LANES),
            vm(LANES, LANES),
            vm(64, 64),
        ],
        [exchange(send)],
    )
    received = exchange(send)
    combined, sums = call(
        row_kernel,
        "rows",
        [struct((LANES, cols), F32), struct((16, cols), F32)],
        [
            vm(4 * cols, LANES),
            vm(2 * cols, LANES),
            vm(2, 1, cols, LANES),
            vm(2, 1, cols, LANES),
            vm(2, 1, 8 * cols, LANES),
            vm(2 * cols, LANES),
            vm(LANES, 2 * cols),
        ],
        [received, vec, high, low],
    )
    out = call(
        lambda *refs: norm_kernel(total_chans, *refs),
        "norm",
        struct(flat, BF16),
        [],
        [combined, sums] + others(sums) + [gate, affine],
    )
    return out.reshape(chans, rows, cols)


def solution(mesh):
    placed = (
        P("ch", "sp", None),
        P("ch", "sp", None),
        P("ch", None),
        P("ch"),
        P(None, None, "ch"),
        P(None, "ch", None),
        P(None, "ch"),
        P(None, "ch", None),
        P(None, "ch"),
        P("ch"),
        P("ch"),
    )
    return jax.shard_map(
        on_device, mesh=mesh, in_specs=placed, out_specs=P("ch", "sp", None), check_vma=False
    )
```

```python
import math

import jax
import jax.numpy as jnp
from jax import lax
from jax.experimental import pallas as pl
from jax.experimental.pallas import tpu as pltpu
from jax.sharding import PartitionSpec as P

F32 = jnp.float32
BF16 = jnp.bfloat16
LANES = 128
EXACT = lax.Precision.HIGHEST
NEG_LOG2E = -1.0 / math.log(2.0)

CHUNK = 8
X_ROWS = 3
BACK = 6
PROJ_PAIRS = 80
VEC_PAIRS = 32


def iota(shape, axis):
    return lax.broadcasted_iota(jnp.int32, shape, axis)


def spread(chans, offset):
    lane = iota((chans, 2 * chans), 1)
    return jnp.where(lane == 2 * iota((chans, 2 * chans), 0) + offset, 1.0, 0.0).astype(F32)


def dup_rows(value, dup):
    return jnp.dot(value, dup, preferred_element_type=F32, precision=EXACT)


def softplus(x):
    return jnp.maximum(x, 0.0) + jnp.log1p(jnp.exp(-jnp.abs(x)))


def silu(x):
    return x * jax.nn.sigmoid(x)


def roll(x, shift, axis):
    return pltpu.roll(x, shift % x.shape[axis], axis)


def start_copies(sources, targets, arrived):
    copies = [
        pltpu.make_async_copy(source, target, arrived.at[index])
        for index, (source, target) in enumerate(zip(sources, targets))
    ]
    for copy in copies:
        copy.start()
    return copies


def prep_kernel(*refs):
    count = 8
    sources, send_ref, scr, vec, near, packed = refs[:count], *refs[count : count + 5]
    loaded, arrived = refs[count + 5 : -1], refs[-1]
    for copy in start_copies(sources, loaded, arrived):
        copy.wait()
    x_ref, cw_ref, cb_ref, pw_ref, dtw_ref, dtb_ref, rate_ref, skip_ref = loaded
    chans = cw_ref.shape[1]
    even, odd = spread(chans, 0), spread(chans, 1)
    even_b, odd_b = even.astype(BF16), odd.astype(BF16)
    half = VEC_PAIRS
    vec[0:9, :] = cw_ref[...]
    vec[9:10, :] = cb_ref[...]
    vec[10:12, :] = dtb_ref[2:4, :]
    vec[12:14, :] = skip_ref[2:4, :]
    vec[14:16, :] = jnp.zeros((2, chans), F32)
    vec[16:24, :] = dtw_ref[2]
    vec[24:32, :] = dtw_ref[3]
    vec[32:48, :] = rate_ref[2]
    vec[48:64, :] = rate_ref[3]
    high = vec[...].astype(BF16)
    low = (vec[0:half, :] - high[0:half].astype(F32)).astype(BF16)
    near[0:16, :] = rate_ref[0]
    near[16:24, :] = dtw_ref[0]
    near[24:25, :] = dtb_ref[0:1, :]
    near[25:26, :] = skip_ref[0:1, :] + skip_ref[1:2, :]
    near[26:32, :] = jnp.zeros((6, chans), F32)
    near[32:48, :] = rate_ref[1]
    near[48:56, :] = dtw_ref[1]
    near[56:57, :] = dtb_ref[1:2, :]
    near[57:64, :] = jnp.zeros((7, chans), F32)
    shared = near[...].astype(BF16)

    def pack(first, second):
        return jnp.dot(first, even_b, preferred_element_type=F32) + jnp.dot(
            second, odd_b, preferred_element_type=F32
        )

    third = pw_ref[2].astype(F32)
    fourth = pw_ref[3].astype(F32)
    rest = jnp.concatenate([third[0:8], fourth[0:8], third[8:40], fourth[8:40]], axis=0)
    packed[0:40, :] = pack(pw_ref[0], rest[0:40].astype(BF16))
    packed[40:80, :] = pack(pw_ref[1], rest[40:80].astype(BF16))
    packed[80:112, :] = pack(high[0:half], high[half:])
    packed[112:128, :] = pack(low[0:16], low[16:])
    packed[128:160, :] = pack(shared[0:half], shared[half:])

    turned = x_ref[...].astype(F32).T
    base = 2 * CHUNK
    scr[pl.ds(base + CHUNK, LANES, stride=CHUNK), :] = turned
    scr[pl.ds(base + 1, LANES, stride=CHUNK), :] = turned
    scr[pl.ds(base - CHUNK + 2, LANES, stride=CHUNK), :] = turned
    scr[base : base + 1, :] = jnp.zeros((1, LANES), F32)
    last = base + CHUNK * (LANES - 1) + 2
    scr[last : last + 1, :] = jnp.zeros((1, LANES), F32)
    slab = lax.axis_index("sp")
    for piece in range(CHUNK - X_ROWS):
        row = packed[pl.ds(32 * piece + slab, 1), :]
        scr[pl.ds(base + X_ROWS + piece, LANES, stride=CHUNK), :] = jnp.broadcast_to(row, (LANES, LANES))
    send_ref[...] = scr[base : base + CHUNK * LANES, :].astype(BF16)


def lane_rows(parts, columns, mask_ref, weights):
    shape = parts.shape
    picked = [
        parts * jnp.broadcast_to(mask_ref[j : j + 1, :], shape).astype(BF16) for j in columns
    ]
    return jnp.dot(jnp.concatenate(picked, axis=0), weights, preferred_element_type=F32)


def scan_pair(steps, rates, delta_ref, drive_ref, expand, wide_ref, part_ref, row_of):
    blocks = delta_ref.shape[1]
    states = [[jnp.zeros((16, LANES), F32) for _ in range(blocks)] for _ in range(2)]

    def prepare(turn):
        for way in range(2):
            first = 8 * turn if way == 0 else steps - 8 - 8 * turn
            for which in range(2):
                wide_ref[way, which, 16 * first : 16 * first + LANES, :] = expand(way, which, first)

    prepare(0)
    for step in range(steps):
        if step % 8 == 0 and step + 8 < steps:
            prepare(step // 8 + 1)
        for way in range(2):
            at = step if way == 0 else steps - 1 - step
            row = row_of(at)
            b_now, c_now = (wide_ref[way, which, 16 * at : 16 * at + 16, :] for which in range(2))
            for block in range(blocks):
                delta = delta_ref[way, block, row : row + 1, :]
                drive = drive_ref[way, block, row : row + 1, :]
                decay = jnp.exp2(delta * rates[way][block])
                state = decay * states[way][block] + drive * b_now
                states[way][block] = state
                product = c_now * state
                part_ref[way, block, 8 * row : 8 * row + 8, :] = product[0:8] + product[8:16]


def outputs_of(part_ref, block, half_ref):
    rows = part_ref.shape[2] // 8
    total = None
    for way in range(2):
        for lane_row in range(4):
            term = part_ref[way, block, pl.ds(lane_row, 2 * rows, stride=4), :]
            total = term if total is None else total + term
    half_ref[0 : 2 * rows, :] = total
    return half_ref[pl.ds(0, rows, stride=2), :] + half_ref[pl.ds(1, rows, stride=2), :]


def halves(value):
    high = value.astype(BF16)
    return high, (value - high.astype(F32)).astype(BF16)


def two_part_dot(value, high, low):
    return jnp.dot(value, high, preferred_element_type=F32) + jnp.dot(
        value, low, preferred_element_type=F32
    )


def row_weights(dtw_ref, dtb_ref, rate_ref, skip_ref, vec_ref, dup):
    for way in range(2):
        vec_ref[16 * way : 16 * way + 16, :] = dup_rows(rate_ref[way], dup) * NEG_LOG2E
        vec_ref[32 + 8 * way : 40 + 8 * way, :] = dup_rows(dtw_ref[way], dup)
    vec_ref[48:52, :] = dup_rows(dtb_ref[...], dup)
    skip = dup_rows(skip_ref[...], dup)
    vec_ref[52:53, :] = skip[0:1] + skip[1:2]
    vec_ref[53:56, :] = jnp.zeros((3, LANES), F32)


def step_weights(vec_refs):
    lane_row = iota((8, LANES), 1) % 2
    columns = []
    for ref in vec_refs:
        for way in range(2):
            dt_rows = ref[32 + 8 * way : 40 + 8 * way, :]
            column = []
            for row in range(2):
                column += [jnp.zeros((40 * way, LANES), F32)] if way else []
                column.append(jnp.where(lane_row == row, dt_rows, 0.0))
                column.append(jnp.zeros((LANES - 40 * way - 8, LANES), F32))
            columns.append(jnp.concatenate(column, axis=0))
    return halves(jnp.concatenate(columns, axis=1))


def column_kernel(recv_ref, *refs):
    count = 7
    sources, outputs = refs[:count], refs[count : count + 7]
    send_ref, own_ref, near_ref, high_ref, low_ref, gate_ref, affine_ref = outputs
    (
        flat_scr,
        back_scr,
        scr,
        delta_scr,
        drive_scr,
        part_scr,
        half_scr,
        mask_scr,
        wide_scr,
    ) = refs[count + 7 : count + 16]
    loaded, arrived = refs[count + 16 : -1], refs[-1]
    copies = start_copies(sources, loaded, arrived)
    slabs = LANES // 4
    pad = 8
    flat_scr[...] = recv_ref[...].astype(F32)
    for row in range(CHUNK):
        scr[row, pad - 4 : pad, :] = jnp.zeros((4, LANES), F32)
        scr[row, pad + LANES : pad + LANES + 4, :] = jnp.zeros((4, LANES), F32)
        scr[row, pad : pad + LANES, :] = flat_scr[pl.ds(row, LANES, stride=CHUNK), :]

    even = iota((slabs, LANES), 1) % 2 == 0
    vecs = []
    projs = []
    conv = []
    for group in range(4):

        def rows_of(row, shift):
            return scr[row, pl.ds(pad + group + 4 * shift, slabs, stride=4), :]

        pieces = [rows_of(row, 0) for row in range(X_ROWS, CHUNK)]
        projs.append([pieces[0], pieces[1], pieces[2][0:16]])
        low = pieces[3][16:32]
        even_16 = even[0:16]
        vec = jnp.concatenate(
            [
                pieces[2][16:32] + jnp.where(even_16, low, 0.0),
                pieces[3][0:16] + jnp.where(even_16, roll(low, -1, 1), 0.0),
            ],
            axis=0,
        )
        vecs.append(vec)
        taps = jnp.where(even[0:16], vec[0:16], roll(vec[0:16], 1, 1))
        total = jnp.zeros((slabs, LANES), F32) + taps[9:10, :]
        for side in range(3):
            here = rows_of(side, 0)
            up = jnp.where(even, roll(rows_of(side, -1), -1, 1), roll(here, 1, 1))
            down = jnp.where(even, roll(here, -1, 1), roll(rows_of(side, 1), 1, 1))
            total = total + taps[side : side + 1, :] * up
            total = total + taps[3 + side : 4 + side, :] * here
            total = total + taps[6 + side : 7 + side, :] * down
        conv.append(silu(total).astype(BF16).astype(F32))

    shared = scr[CHUNK - 1, pl.ds(pad + (lax.axis_index("ch") ^ 2), slabs, stride=4), :]
    for way, value in enumerate(
        (jnp.where(even, shared, roll(shared, 1, 1)), jnp.where(even, roll(shared, -1, 1), shared))
    ):
        near_ref[16 * way : 16 * way + 16, :] = value[0:16] * NEG_LOG2E
        near_ref[32 + 8 * way : 40 + 8 * way, :] = value[16:24]
        near_ref[48 + way : 49 + way, :] = value[24:25]
        if way == 0:
            near_ref[52:53, :] = value[25:26]
    near_ref[50:52, :] = jnp.zeros((2, LANES), F32)
    near_ref[53:56, :] = jnp.zeros((3, LANES), F32)

    def from_even(left, right):
        mask = iota(left.shape, 1) % 2 == 0
        return jnp.where(mask, left, roll(right, 1, 1))

    def from_odd(left, right):
        mask = iota(left.shape, 1) % 2 == 0
        return jnp.where(mask, roll(left, -1, 1), right)

    def all_groups(take, parts):
        return jnp.concatenate([take(parts[0], parts[1]), take(parts[2], parts[3])], axis=1)

    values = jnp.concatenate([all_groups(from_even, conv), all_groups(from_odd, conv)], axis=0)
    values_b = values.astype(BF16)
    proj_w = jnp.concatenate(
        [
            all_groups(take, [p[piece] for p in projs])
            for take in (from_even, from_odd)
            for piece in range(3)
        ],
        axis=0,
    ).astype(BF16)
    vec = jnp.concatenate([all_groups(from_even, vecs), all_groups(from_odd, vecs)], axis=0)

    nt = (((1,), (1,)), ((), ()))
    proj = lax.dot_general(values_b, proj_w[0:128], nt, preferred_element_type=F32)
    proj = proj.astype(BF16).astype(F32)
    turned = lax.dot_general(proj_w[96:160], values_b, nt, preferred_element_type=F32)
    turned = turned.astype(BF16)

    low = lax.dot_general(values_b, proj_w[80:96], nt, preferred_element_type=F32).astype(BF16)
    dt_rows = vec[16:32]
    second_half = iota((16, 256), 0) >= 8
    rates = []
    for way in range(2):
        chosen = jnp.where(second_half == (way == 1), dt_rows, 0.0)
        delta = softplus(two_part_dot(low, *halves(chosen)) + vec[10 + way : 11 + way, :])
        drive = delta * values
        scaled = vec[32 + 16 * way : 48 + 16 * way] * NEG_LOG2E
        rates.append([scaled[:, 0:LANES], scaled[:, LANES:]])
        for block in range(2):
            lanes = slice(LANES * block, LANES * block + LANES)
            delta_scr[way, block] = delta[:, lanes]
            drive_scr[way, block] = drive[:, lanes]

    def row_of(at):
        return (at % 2) * slabs + at // 2

    mask_scr[...] = jnp.where(iota((64, 64), 0) == iota((64, 64), 1), 1.0, 0.0)
    ones = jnp.ones((64, LANES), BF16)

    def expand(way, which, first):
        parts = turned[32 * way + 16 * which : 32 * way + 16 * which + 16]
        return lane_rows(parts, [row_of(first + j) for j in range(8)], mask_scr, ones)

    scan_pair(2 * slabs, rates, delta_scr, drive_scr, expand, wide_scr, part_scr, row_of)

    for copy in copies:
        copy.wait()
    dtw_ref, dtb_ref, rate_ref, skip_ref, gain_ref, bias_ref, gate_in_ref = loaded
    chans = dtw_ref.shape[2]
    dup = spread(chans, 0) + spread(chans, 1)
    row_weights(dtw_ref, dtb_ref, rate_ref, skip_ref, own_ref, dup)
    high_ref[...], low_ref[...] = step_weights((own_ref, near_ref))
    gate_ref[...] = silu(gate_in_ref[...].astype(F32))
    pick = iota((LANES, LANES), 0) == iota((LANES, LANES), 1)
    for index, ref in enumerate((gain_ref, bias_ref)):
        column = jnp.sum(jnp.where(pick, dup_rows(ref[...], dup), 0.0), axis=1, keepdims=True)
        affine_ref[index] = jnp.broadcast_to(column, (LANES, LANES))

    skip = vec[12:13] + vec[13:14]
    backs = []
    for block in range(2):
        lanes = slice(LANES * block, LANES * block + LANES)
        y = outputs_of(part_scr, block, half_scr) + skip[:, lanes] * values[:, lanes]
        y_even, y_odd = y[0:slabs], y[slabs:]
        backs.append(jnp.where(even, y_even, roll(y_odd, 1, 1)))
        backs.append(jnp.where(even, roll(y_even, -1, 1), y_odd))
    for group in range(4):
        near = group ^ 2
        parts = (backs[group], conv[group], proj[0:slabs], proj[slabs:], backs[near], conv[near])
        for row, value in enumerate(parts):
            scr[row, pl.ds(group, slabs, stride=4), :] = value
    for row in range(BACK):
        back_scr[pl.ds(row, LANES, stride=BACK), :] = scr[row, 0:LANES, :]
    send_ref[...] = back_scr[...].astype(BF16)


def row_kernel(
    recv_ref,
    own_ref,
    near_ref,
    high_ref,
    low_ref,
    comb_ref,
    sums_ref,
    scr,
    mixed_scr,
    delta_scr,
    drive_scr,
    part_scr,
    half_scr,
    mask_scr,
    wide_scr,
):
    cols = LANES
    scr[...] = recv_ref[...].astype(F32)

    def chunk_row(row):
        return scr[pl.ds(row, cols, stride=BACK), :]

    proj = [chunk_row(2), chunk_row(3)]
    both = jnp.concatenate(proj, axis=1).astype(BF16)
    low_rank = two_part_dot(both, high_ref[...], low_ref[...])
    vecs = (own_ref, near_ref)
    verticals = (chunk_row(0), chunk_row(4))
    values = (chunk_row(1), chunk_row(5))
    for block in range(2):
        for way in range(2):
            first = LANES * (2 * block + way)
            delta = softplus(
                low_rank[:, first : first + LANES] + vecs[block][48 + way : 49 + way, :]
            )
            delta_scr[way, block] = delta
            drive_scr[way, block] = delta * values[block]
    rates = [[vec[16 * way : 16 * way + 16, :] for vec in vecs] for way in range(2)]

    for row in range(2):
        mixed_scr[pl.ds(row, cols, stride=2), :] = proj[row]
    turned = mixed_scr[...].T
    mask_scr[...] = jnp.where(iota((64, LANES), 1) // 2 == iota((64, LANES), 0), 1.0, 0.0)
    alike = iota((LANES, LANES), 0) % 2 == iota((LANES, LANES), 1) % 2
    by_row = jnp.where(alike, 1.0, 0.0).astype(BF16)

    def expand(way, which, first):
        top = 40 * way + 8 + 16 * which
        start = LANES * (first // 64)
        parts = turned[top : top + 16, start : start + LANES].astype(BF16)
        return lane_rows(parts, [(first + j) % 64 for j in range(8)], mask_scr, by_row)

    scan_pair(cols, rates, delta_scr, drive_scr, expand, wide_scr, part_scr, lambda at: at)
    sums = [jnp.zeros((8, LANES), F32) for _ in range(2)]
    for block in range(2):
        combined = (
            outputs_of(part_scr, block, half_scr)
            + vecs[block][52:53, :] * values[block]
            + verticals[block]
        )
        combined = combined.T
        if block == 0:
            comb_ref[...] = combined
        for tile in range(LANES // 8):
            rows = combined[8 * tile : 8 * tile + 8]
            sums = [sums[0] + rows, sums[1] + rows * rows]
    for index, value in enumerate(sums):
        value = value + roll(value, 4, 0)
        value = value + roll(value, 2, 0)
        sums_ref[8 * index : 8 * index + 8, :] = value


def norm_kernel(total_chans, comb_ref, s0_ref, s1_ref, gate_ref, affine_ref, out_ref):
    sums = s0_ref[...] + s1_ref[...]
    mean = sums[0:8] / total_chans
    var = sums[8:16] / total_chans - mean * mean
    scale = lax.rsqrt(var + 1e-05)
    comb = comb_ref[...]
    means = jnp.concatenate([mean] * (LANES // 8), axis=0)
    scales = jnp.concatenate([scale] * (LANES // 8), axis=0)
    normed = (comb - means) * scales * affine_ref[0] + affine_ref[1]
    out_ref[...] = (normed * gate_ref[...]).astype(BF16)


VMEM = pl.BlockSpec(memory_space=pltpu.VMEM)


def call(kernel, name, outs, scratch, inputs, place=VMEM, grant=24 << 20):
    single = not isinstance(outs, (list, tuple))
    return pl.pallas_call(
        kernel,
        out_shape=outs,
        in_specs=place if isinstance(place, list) else [place] * len(inputs),
        out_specs=VMEM if single else [VMEM] * len(outs),
        scratch_shapes=scratch,
        name=name,
        compiler_params=pltpu.CompilerParams(vmem_limit_bytes=grant),
    )(*inputs)


def other(value, flip):
    return lax.ppermute(value, "ch", [(i, i ^ flip) for i in range(lax.axis_size("ch"))])


def exchange(value, chunk, tile):
    peers = value.shape[0] // chunk
    pieces = value.reshape(peers, chunk // tile, tile, LANES)
    moved = lax.all_to_all(pieces, ("sp", "ch"), split_axis=0, concat_axis=0, tiled=True)
    return moved.reshape(value.shape)


def on_device(
    x_in,
    gate_in,
    conv_weight,
    conv_bias,
    proj_weight,
    dt_weight,
    dt_bias,
    decay_rate,
    skip_gain,
    norm_gain,
    norm_bias,
):
    chans, rows, cols = x_in.shape
    total_chans = chans * lax.axis_size("ch")
    flat = (chans * rows, cols)
    struct = jax.ShapeDtypeStruct

    def vm(*shape):
        return pltpu.VMEM(shape, F32)

    dt_weight = dt_weight.transpose(0, 2, 1)
    decay_rate = decay_rate.transpose(0, 2, 1)
    arguments = [
        x_in.reshape(flat),
        conv_weight.T,
        conv_bias.reshape(1, chans),
        proj_weight,
        dt_weight,
        dt_bias,
        decay_rate,
        skip_gain,
    ]
    send = call(
        prep_kernel,
        "prep",
        struct((CHUNK * cols, LANES), BF16),
        [vm(CHUNK * (cols + 4), LANES), vm(2 * VEC_PAIRS, chans), vm(64, chans), vm(160, LANES)]
        + [pltpu.VMEM(value.shape, value.dtype) for value in arguments]
        + [pltpu.SemaphoreType.DMA((len(arguments),))],
        [pltpu.with_memory_space_constraint(value, pltpu.HBM) for value in arguments],
        pl.BlockSpec(memory_space=pltpu.HBM),
    )
    hbm = pl.BlockSpec(memory_space=pltpu.HBM)
    arguments = [
        pltpu.with_memory_space_constraint(value, pltpu.HBM)
        for value in (
            dt_weight,
            dt_bias,
            decay_rate,
            skip_gain,
            norm_gain.reshape(1, chans),
            norm_bias.reshape(1, chans),
            gate_in.reshape(flat),
        )
    ]
    send, own, near, high, low, gate, affine = call(
        column_kernel,
        "columns",
        [
            struct((BACK * cols, LANES), BF16),
            struct((56, LANES), F32),
            struct((56, LANES), F32),
            struct((2 * LANES, 4 * LANES), BF16),
            struct((2 * LANES, 4 * LANES), BF16),
            struct((LANES, cols), F32),
            struct((2, LANES, cols), F32),
        ],
        [
            vm(CHUNK * cols, LANES),
            vm(BACK * cols, LANES),
            vm(CHUNK, cols + 16, LANES),
            vm(2, 2, 64, LANES),
            vm(2, 2, 64, LANES),
            vm(2, 2, 8 * 64, LANES),
            vm(LANES, LANES),
            vm(64, 64),
            vm(2, 2, 16 * 64, LANES),
        ]
        + [pltpu.VMEM(value.shape, value.dtype) for value in arguments]
        + [pltpu.SemaphoreType.DMA((len(arguments),))],
        [exchange(send, CHUNK, CHUNK)] + arguments,
        [VMEM] + [hbm] * len(arguments),
    )
    received = exchange(send, BACK, 2)
    combined, sums = call(
        row_kernel,
        "rows",
        [struct((LANES, cols), F32), struct((16, cols), F32)],
        [
            vm(BACK * cols, LANES),
            vm(2 * cols, LANES),
            vm(2, 2, cols, LANES),
            vm(2, 2, cols, LANES),
            vm(2, 2, 8 * cols, LANES),
            vm(2 * cols, LANES),
            vm(64, LANES),
            vm(2, 2, 16 * cols, LANES),
        ],
        [received, own, near, high, low],
    )
    out = call(
        lambda *refs: norm_kernel(total_chans, *refs),
        "norm",
        struct(flat, BF16),
        [],
        [combined, sums, other(sums, 1), gate, affine],
    )
    return out.reshape(chans, rows, cols)


def solution(mesh):
    placed = (
        P("ch", "sp", None),
        P("ch", "sp", None),
        P("ch", None),
        P("ch"),
        P(None, None, "ch"),
        P(None, "ch", None),
        P(None, "ch"),
        P(None, "ch", None),
        P(None, "ch"),
        P("ch"),
        P("ch"),
    )
    return jax.shard_map(
        on_device, mesh=mesh, in_specs=placed, out_specs=P("ch", "sp", None), check_vma=False
    )
```

```python
import math

import jax
import jax.numpy as jnp
from jax import lax
from jax.experimental import pallas as pl
from jax.experimental.pallas import tpu as pltpu
from jax.sharding import PartitionSpec as P

F32 = jnp.float32
BF16 = jnp.bfloat16
LANES = 128
EXACT = lax.Precision.HIGHEST
NEG_LOG2E = -1.0 / math.log(2.0)

CHUNK = 8
X_ROWS = 3
BACK = 6
PROJ_PAIRS = 80
VEC_PAIRS = 32


def iota(shape, axis):
    return lax.broadcasted_iota(jnp.int32, shape, axis)


def spread(chans, offset):
    lane = iota((chans, 2 * chans), 1)
    return jnp.where(lane == 2 * iota((chans, 2 * chans), 0) + offset, 1.0, 0.0).astype(F32)


def dup_rows(value, dup):
    return jnp.dot(value, dup, preferred_element_type=F32, precision=EXACT)


def softplus(x):
    return jnp.maximum(x, 0.0) + jnp.log(1.0 + jnp.exp(-jnp.abs(x)))


def silu(x):
    return x * jax.nn.sigmoid(x)


def roll(x, shift, axis):
    return pltpu.roll(x, shift % x.shape[axis], axis)


def start_copies(sources, targets, arrived):
    copies = [
        pltpu.make_async_copy(source, target, arrived.at[index])
        for index, (source, target) in enumerate(zip(sources, targets))
    ]
    for copy in copies:
        copy.start()
    return copies


def prep_kernel(*refs):
    count, kept = 11, 7
    sources, send_ref, col_mask_ref, row_mask_ref = refs[:count], *refs[count : count + 3]
    handed = refs[count + 3 : count + 3 + kept]
    scr, vec, near, packed, *own, arrived = refs[count + 3 + kept :]
    loaded = (*own, *handed)
    copies = start_copies(sources, loaded, arrived)
    for j in range(64):
        rows = slice(16 * j, 16 * j + 16)
        lane = iota((16, LANES), 1)
        col_mask_ref[rows, :] = jnp.where(lane[:, 0:64] == j, 1.0, 0.0).astype(BF16)
        row_mask_ref[rows, :] = jnp.where(lane // 2 == j, 1.0, 0.0).astype(BF16)
    for copy in copies:
        copy.wait()
    x_ref, cw_ref, cb_ref, pw_ref, dtw_ref, dtb_ref, rate_ref, skip_ref = loaded[:8]
    chans = cw_ref.shape[1]
    even, odd = spread(chans, 0), spread(chans, 1)
    even_b, odd_b = even.astype(BF16), odd.astype(BF16)
    half = VEC_PAIRS
    vec[0:9, :] = cw_ref[...]
    vec[9:10, :] = cb_ref[...]
    vec[10:12, :] = dtb_ref[2:4, :]
    vec[12:14, :] = skip_ref[2:4, :]
    vec[14:16, :] = jnp.zeros((2, chans), F32)
    vec[16:24, :] = dtw_ref[2]
    vec[24:32, :] = dtw_ref[3]
    vec[32:48, :] = rate_ref[2]
    vec[48:64, :] = rate_ref[3]
    high = vec[...].astype(BF16)
    low = (vec[0:half, :] - high[0:half].astype(F32)).astype(BF16)
    near[0:16, :] = rate_ref[0]
    near[16:24, :] = dtw_ref[0]
    near[24:25, :] = dtb_ref[0:1, :]
    near[25:26, :] = skip_ref[0:1, :] + skip_ref[1:2, :]
    near[26:32, :] = jnp.zeros((6, chans), F32)
    near[32:48, :] = rate_ref[1]
    near[48:56, :] = dtw_ref[1]
    near[56:57, :] = dtb_ref[1:2, :]
    near[57:64, :] = jnp.zeros((7, chans), F32)
    shared = near[...].astype(BF16)

    def pack(first, second):
        return jnp.dot(first, even_b, preferred_element_type=F32) + jnp.dot(
            second, odd_b, preferred_element_type=F32
        )

    third = pw_ref[2].astype(F32)
    fourth = pw_ref[3].astype(F32)
    rest = jnp.concatenate([third[0:8], fourth[0:8], third[8:40], fourth[8:40]], axis=0)
    packed[0:40, :] = pack(pw_ref[0], rest[0:40].astype(BF16))
    packed[40:80, :] = pack(pw_ref[1], rest[40:80].astype(BF16))
    packed[80:112, :] = pack(high[0:half], high[half:])
    packed[112:128, :] = pack(low[0:16], low[16:])
    packed[128:160, :] = pack(shared[0:half], shared[half:])

    turned = x_ref[...].astype(F32).T
    base = 2 * CHUNK
    scr[pl.ds(base + CHUNK, LANES, stride=CHUNK), :] = turned
    scr[pl.ds(base + 1, LANES, stride=CHUNK), :] = turned
    scr[pl.ds(base - CHUNK + 2, LANES, stride=CHUNK), :] = turned
    scr[base : base + 1, :] = jnp.zeros((1, LANES), F32)
    last = base + CHUNK * (LANES - 1) + 2
    scr[last : last + 1, :] = jnp.zeros((1, LANES), F32)
    slab = lax.axis_index("sp")
    for piece in range(CHUNK - X_ROWS):
        row = packed[pl.ds(32 * piece + slab, 1), :]
        scr[pl.ds(base + X_ROWS + piece, LANES, stride=CHUNK), :] = jnp.broadcast_to(row, (LANES, LANES))
    send_ref[...] = scr[base : base + CHUNK * LANES, :].astype(BF16)


def lane_rows(parts, columns, mask_ref, weights):
    picked = [parts * mask_ref[16 * j : 16 * j + 16, :] for j in columns]
    return jnp.dot(jnp.concatenate(picked, axis=0), weights, preferred_element_type=F32)


def scan_pair(steps, rates, delta_ref, drive_ref, expand, wide_ref, part_ref, row_of):
    blocks = delta_ref.shape[1]
    states = [[jnp.zeros((16, LANES), F32) for _ in range(blocks)] for _ in range(2)]

    def prepare(turn):
        for way in range(2):
            first = 8 * turn if way == 0 else steps - 8 - 8 * turn
            for which in range(2):
                wide_ref[way, which, 16 * first : 16 * first + LANES, :] = expand(way, which, first)

    prepare(0)
    for step in range(steps):
        if step % 8 == 0 and step + 8 < steps:
            prepare(step // 8 + 1)
        for way in range(2):
            at = step if way == 0 else steps - 1 - step
            row = row_of(at)
            b_now, c_now = (wide_ref[way, which, 16 * at : 16 * at + 16, :] for which in range(2))
            for block in range(blocks):
                delta = delta_ref[way, block, row : row + 1, :]
                drive = drive_ref[way, block, row : row + 1, :]
                decay = jnp.exp2(delta * rates[way][block])
                state = decay * states[way][block] + drive * b_now
                states[way][block] = state
                product = c_now * state
                part_ref[way, block, 8 * row : 8 * row + 8, :] = product[0:8] + product[8:16]


def outputs_of(part_ref, block, half_ref):
    rows = part_ref.shape[2] // 8
    total = None
    for way in range(2):
        for lane_row in range(4):
            term = part_ref[way, block, pl.ds(lane_row, 2 * rows, stride=4), :]
            total = term if total is None else total + term
    half_ref[0 : 2 * rows, :] = total
    return half_ref[pl.ds(0, rows, stride=2), :] + half_ref[pl.ds(1, rows, stride=2), :]


def halves(value):
    high = value.astype(BF16)
    return high, (value - high.astype(F32)).astype(BF16)


def two_part_dot(value, high, low):
    return jnp.dot(value, high, preferred_element_type=F32) + jnp.dot(
        value, low, preferred_element_type=F32
    )


def row_weights(dtw_ref, dtb_ref, rate_ref, skip_ref, vec_ref, dup):
    for way in range(2):
        vec_ref[16 * way : 16 * way + 16, :] = dup_rows(rate_ref[way], dup) * NEG_LOG2E
        vec_ref[32 + 8 * way : 40 + 8 * way, :] = dup_rows(dtw_ref[way], dup)
    vec_ref[48:52, :] = dup_rows(dtb_ref[...], dup)
    skip = dup_rows(skip_ref[...], dup)
    vec_ref[52:53, :] = skip[0:1] + skip[1:2]
    vec_ref[53:56, :] = jnp.zeros((3, LANES), F32)


def step_weights(vec_refs):
    lane_row = iota((8, LANES), 1) % 2
    columns = []
    for ref in vec_refs:
        for way in range(2):
            dt_rows = ref[32 + 8 * way : 40 + 8 * way, :]
            column = []
            for row in range(2):
                column += [jnp.zeros((40 * way, LANES), F32)] if way else []
                column.append(jnp.where(lane_row == row, dt_rows, 0.0))
                column.append(jnp.zeros((LANES - 40 * way - 8, LANES), F32))
            columns.append(jnp.concatenate(column, axis=0))
    return halves(jnp.concatenate(columns, axis=1))


def column_kernel(
    recv_ref,
    mask_ref,
    dtw_ref,
    dtb_ref,
    rate_ref,
    skip_ref,
    gain_ref,
    bias_ref,
    gate_in_ref,
    send_ref,
    own_ref,
    near_ref,
    high_ref,
    low_ref,
    gate_ref,
    affine_ref,
    flat_scr,
    back_scr,
    scr,
    swap_scr,
    delta_scr,
    drive_scr,
    part_scr,
    half_scr,
    wide_scr,
):
    slabs = LANES // 4
    pad = 8
    flat_scr[...] = recv_ref[...].astype(F32)
    swapped = iota((LANES, LANES), 1) ^ 1
    for row in range(CHUNK):
        value = flat_scr[pl.ds(row, LANES, stride=CHUNK), :]
        scr[row] = value
        if row < X_ROWS:
            swap_scr[row, pad - 4 : pad, :] = jnp.zeros((4, LANES), F32)
            swap_scr[row, pad + LANES : pad + LANES + 4, :] = jnp.zeros((4, LANES), F32)
            swap_scr[row, pad : pad + LANES, :] = jnp.take_along_axis(
                value, swapped, axis=1, mode="promise_in_bounds"
            )

    even = iota((slabs, LANES), 1) % 2 == 0
    vecs = []
    projs = []
    conv = []
    for group in range(4):

        def rows_of(row):
            return scr[row, pl.ds(group, slabs, stride=4), :]

        def swapped_of(row, shift):
            return swap_scr[row, pl.ds(pad + group + 4 * shift, slabs, stride=4), :]

        pieces = [rows_of(row) for row in range(X_ROWS, CHUNK)]
        projs.append([pieces[0], pieces[1], pieces[2][0:16]])
        low = pieces[3][16:32]
        even_16 = even[0:16]
        vec = jnp.concatenate(
            [
                pieces[2][16:32] + jnp.where(even_16, low, 0.0),
                pieces[3][0:16] + jnp.where(even_16, roll(low, -1, 1), 0.0),
            ],
            axis=0,
        )
        vecs.append(vec)
        taps = jnp.where(even[0:16], vec[0:16], roll(vec[0:16], 1, 1))
        total = jnp.zeros((slabs, LANES), F32) + taps[9:10, :]
        for side in range(3):
            above, below = taps[side : side + 1, :], taps[6 + side : 7 + side, :]
            beyond = jnp.where(even, swapped_of(side, -1), swapped_of(side, 1))
            total = total + jnp.where(even[0:1], above, below) * beyond
            total = total + jnp.where(even[0:1], below, above) * swapped_of(side, 0)
            total = total + taps[3 + side : 4 + side, :] * rows_of(side)
        conv.append(silu(total).astype(BF16).astype(F32))

    shared = scr[CHUNK - 1, pl.ds(lax.axis_index("ch") ^ 2, slabs, stride=4), :]
    for way, value in enumerate(
        (jnp.where(even, shared, roll(shared, 1, 1)), jnp.where(even, roll(shared, -1, 1), shared))
    ):
        near_ref[16 * way : 16 * way + 16, :] = value[0:16] * NEG_LOG2E
        near_ref[32 + 8 * way : 40 + 8 * way, :] = value[16:24]
        near_ref[48 + way : 49 + way, :] = value[24:25]
        if way == 0:
            near_ref[52:53, :] = value[25:26]
    near_ref[50:52, :] = jnp.zeros((2, LANES), F32)
    near_ref[53:56, :] = jnp.zeros((3, LANES), F32)

    chans = dtw_ref.shape[2]
    dup = spread(chans, 0) + spread(chans, 1)
    row_weights(dtw_ref, dtb_ref, rate_ref, skip_ref, own_ref, dup)
    high_ref[...], low_ref[...] = step_weights((own_ref, near_ref))
    gate_ref[...] = silu(gate_in_ref[...].astype(F32))
    pick = iota((LANES, LANES), 0) == iota((LANES, LANES), 1)
    for index, ref in enumerate((gain_ref, bias_ref)):
        column = jnp.sum(jnp.where(pick, dup_rows(ref[...], dup), 0.0), axis=1, keepdims=True)
        affine_ref[index] = jnp.broadcast_to(column, (LANES, LANES))

    def from_even(left, right):
        mask = iota(left.shape, 1) % 2 == 0
        return jnp.where(mask, left, roll(right, 1, 1))

    def from_odd(left, right):
        mask = iota(left.shape, 1) % 2 == 0
        return jnp.where(mask, roll(left, -1, 1), right)

    def all_groups(take, parts):
        return jnp.concatenate([take(parts[0], parts[1]), take(parts[2], parts[3])], axis=1)

    values = jnp.concatenate([all_groups(from_even, conv), all_groups(from_odd, conv)], axis=0)
    values_b = values.astype(BF16)
    proj_w = jnp.concatenate(
        [
            all_groups(take, [p[piece] for p in projs])
            for take in (from_even, from_odd)
            for piece in range(3)
        ],
        axis=0,
    ).astype(BF16)
    vec = jnp.concatenate([all_groups(from_even, vecs), all_groups(from_odd, vecs)], axis=0)

    nt = (((1,), (1,)), ((), ()))
    proj = lax.dot_general(values_b, proj_w[0:128], nt, preferred_element_type=F32)
    proj = proj.astype(BF16).astype(F32)
    turned = lax.dot_general(proj_w[96:160], values_b, nt, preferred_element_type=F32)
    turned = turned.astype(BF16)

    low = lax.dot_general(values_b, proj_w[80:96], nt, preferred_element_type=F32).astype(BF16)
    dt_rows = vec[16:32]
    second_half = iota((16, 256), 0) >= 8
    rates = []
    for way in range(2):
        chosen = jnp.where(second_half == (way == 1), dt_rows, 0.0)
        delta = softplus(two_part_dot(low, *halves(chosen)) + vec[10 + way : 11 + way, :])
        drive = delta * values
        scaled = vec[32 + 16 * way : 48 + 16 * way] * NEG_LOG2E
        rates.append([scaled[:, 0:LANES], scaled[:, LANES:]])
        for block in range(2):
            lanes = slice(LANES * block, LANES * block + LANES)
            delta_scr[way, block] = delta[:, lanes]
            drive_scr[way, block] = drive[:, lanes]

    def row_of(at):
        return (at % 2) * slabs + at // 2

    ones = jnp.ones((64, LANES), BF16)

    def expand(way, which, first):
        parts = turned[32 * way + 16 * which : 32 * way + 16 * which + 16]
        return lane_rows(parts, [row_of(first + j) for j in range(8)], mask_ref, ones)

    scan_pair(2 * slabs, rates, delta_scr, drive_scr, expand, wide_scr, part_scr, row_of)

    skip = vec[12:13] + vec[13:14]
    backs = []
    for block in range(2):
        lanes = slice(LANES * block, LANES * block + LANES)
        y = outputs_of(part_scr, block, half_scr) + skip[:, lanes] * values[:, lanes]
        y_even, y_odd = y[0:slabs], y[slabs:]
        backs.append(jnp.where(even, y_even, roll(y_odd, 1, 1)))
        backs.append(jnp.where(even, roll(y_even, -1, 1), y_odd))
    for group in range(4):
        near = group ^ 2
        parts = (backs[group], conv[group], proj[0:slabs], proj[slabs:], backs[near], conv[near])
        for row, value in enumerate(parts):
            scr[row, pl.ds(group, slabs, stride=4), :] = value
    for row in range(BACK):
        back_scr[pl.ds(row, LANES, stride=BACK), :] = scr[row, 0:LANES, :]
    send_ref[...] = back_scr[...].astype(BF16)


def row_kernel(
    recv_ref,
    mask_ref,
    own_ref,
    near_ref,
    high_ref,
    low_ref,
    comb_ref,
    sums_ref,
    scr,
    mixed_scr,
    delta_scr,
    drive_scr,
    part_scr,
    half_scr,
    wide_scr,
):
    cols = LANES
    scr[...] = recv_ref[...].astype(F32)

    def chunk_row(row):
        return scr[pl.ds(row, cols, stride=BACK), :]

    proj = [chunk_row(2), chunk_row(3)]
    both = jnp.concatenate(proj, axis=1).astype(BF16)
    low_rank = two_part_dot(both, high_ref[...], low_ref[...])
    vecs = (own_ref, near_ref)
    verticals = (chunk_row(0), chunk_row(4))
    values = (chunk_row(1), chunk_row(5))
    for block in range(2):
        for way in range(2):
            first = LANES * (2 * block + way)
            delta = softplus(
                low_rank[:, first : first + LANES] + vecs[block][48 + way : 49 + way, :]
            )
            delta_scr[way, block] = delta
            drive_scr[way, block] = delta * values[block]
    rates = [[vec[16 * way : 16 * way + 16, :] for vec in vecs] for way in range(2)]

    for row in range(2):
        mixed_scr[pl.ds(row, cols, stride=2), :] = proj[row]
    turned = mixed_scr[...].T
    alike = iota((LANES, LANES), 0) % 2 == iota((LANES, LANES), 1) % 2
    by_row = jnp.where(alike, 1.0, 0.0).astype(BF16)

    def expand(way, which, first):
        top = 40 * way + 8 + 16 * which
        start = LANES * (first // 64)
        parts = turned[top : top + 16, start : start + LANES].astype(BF16)
        return lane_rows(parts, [(first + j) % 64 for j in range(8)], mask_ref, by_row)

    scan_pair(cols, rates, delta_scr, drive_scr, expand, wide_scr, part_scr, lambda at: at)
    sums = [jnp.zeros((8, LANES), F32) for _ in range(2)]
    for block in range(2):
        combined = (
            outputs_of(part_scr, block, half_scr)
            + vecs[block][52:53, :] * values[block]
            + verticals[block]
        )
        combined = combined.T
        if block == 0:
            comb_ref[...] = combined
        for tile in range(LANES // 8):
            rows = combined[8 * tile : 8 * tile + 8]
            sums = [sums[0] + rows, sums[1] + rows * rows]
    for index, value in enumerate(sums):
        value = value + roll(value, 4, 0)
        value = value + roll(value, 2, 0)
        sums_ref[8 * index : 8 * index + 8, :] = value


def norm_kernel(total_chans, comb_ref, s0_ref, s1_ref, gate_ref, affine_ref, out_ref):
    sums = s0_ref[...] + s1_ref[...]
    mean = sums[0:8] / total_chans
    var = sums[8:16] / total_chans - mean * mean
    scale = lax.rsqrt(var + 1e-05)
    comb = comb_ref[...]
    means = jnp.concatenate([mean] * (LANES // 8), axis=0)
    scales = jnp.concatenate([scale] * (LANES // 8), axis=0)
    normed = (comb - means) * scales * affine_ref[0] + affine_ref[1]
    out_ref[...] = (normed * gate_ref[...]).astype(BF16)


VMEM = pl.BlockSpec(memory_space=pltpu.VMEM)


def call(kernel, name, outs, scratch, inputs, place=VMEM, grant=24 << 20):
    single = not isinstance(outs, (list, tuple))
    return pl.pallas_call(
        kernel,
        out_shape=outs,
        in_specs=[place] * len(inputs),
        out_specs=VMEM if single else [VMEM] * len(outs),
        scratch_shapes=scratch,
        name=name,
        compiler_params=pltpu.CompilerParams(vmem_limit_bytes=grant),
    )(*inputs)


def other(value, flip):
    return lax.ppermute(value, "ch", [(i, i ^ flip) for i in range(lax.axis_size("ch"))])


def exchange(value, chunk, tile):
    peers = value.shape[0] // chunk
    pieces = value.reshape(peers, chunk // tile, tile, LANES)
    moved = lax.all_to_all(pieces, ("sp", "ch"), split_axis=0, concat_axis=0, tiled=True)
    return moved.reshape(value.shape)


def on_device(
    x_in,
    gate_in,
    conv_weight,
    conv_bias,
    proj_weight,
    dt_weight,
    dt_bias,
    decay_rate,
    skip_gain,
    norm_gain,
    norm_bias,
):
    chans, rows, cols = x_in.shape
    total_chans = chans * lax.axis_size("ch")
    flat = (chans * rows, cols)
    struct = jax.ShapeDtypeStruct

    def vm(*shape):
        return pltpu.VMEM(shape, F32)

    dt_weight = dt_weight.transpose(0, 2, 1)
    decay_rate = decay_rate.transpose(0, 2, 1)
    arguments = [
        pltpu.with_memory_space_constraint(value, pltpu.HBM)
        for value in (
            x_in.reshape(flat),
            conv_weight.T,
            conv_bias.reshape(1, chans),
            proj_weight,
            dt_weight,
            dt_bias,
            decay_rate,
            skip_gain,
            norm_gain.reshape(1, chans),
            norm_bias.reshape(1, chans),
            gate_in.reshape(flat),
        )
    ]
    send, col_mask, row_mask, *handed = call(
        prep_kernel,
        "prep",
        [
            struct((CHUNK * cols, LANES), BF16),
            struct((64 * 16, 64), BF16),
            struct((64 * 16, LANES), BF16),
        ]
        + [struct(value.shape, value.dtype) for value in arguments[4:]],
        [
            vm(CHUNK * (cols + 4), LANES),
            vm(2 * VEC_PAIRS, chans),
            vm(64, chans),
            vm(160, LANES),
        ]
        + [pltpu.VMEM(value.shape, value.dtype) for value in arguments[:4]]
        + [pltpu.SemaphoreType.DMA((len(arguments),))],
        arguments,
        pl.BlockSpec(memory_space=pltpu.HBM),
    )
    send, own, near, high, low, gate, affine = call(
        column_kernel,
        "columns",
        [
            struct((BACK * cols, LANES), BF16),
            struct((56, LANES), F32),
            struct((56, LANES), F32),
            struct((2 * LANES, 4 * LANES), BF16),
            struct((2 * LANES, 4 * LANES), BF16),
            struct((LANES, cols), F32),
            struct((2, LANES, cols), F32),
        ],
        [
            vm(CHUNK * cols, LANES),
            vm(BACK * cols, LANES),
            vm(CHUNK, cols, LANES),
            vm(X_ROWS, cols + 16, LANES),
            vm(2, 2, 64, LANES),
            vm(2, 2, 64, LANES),
            vm(2, 2, 8 * 64, LANES),
            vm(LANES, LANES),
            vm(2, 2, 16 * 64, LANES),
        ],
        [exchange(send, CHUNK, CHUNK), col_mask] + handed,
    )
    received = exchange(send, BACK, 2)
    combined, sums = call(
        row_kernel,
        "rows",
        [struct((LANES, cols), F32), struct((16, cols), F32)],
        [
            vm(BACK * cols, LANES),
            vm(2 * cols, LANES),
            vm(2, 2, cols, LANES),
            vm(2, 2, cols, LANES),
            vm(2, 2, 8 * cols, LANES),
            vm(2 * cols, LANES),
            vm(2, 2, 16 * cols, LANES),
        ],
        [received, row_mask, own, near, high, low],
    )
    out = call(
        lambda *refs: norm_kernel(total_chans, *refs),
        "norm",
        struct(flat, BF16),
        [],
        [combined, sums, other(sums, 1), gate, affine],
    )
    return out.reshape(chans, rows, cols)


def solution(mesh):
    placed = (
        P("ch", "sp", None),
        P("ch", "sp", None),
        P("ch", None),
        P("ch"),
        P(None, None, "ch"),
        P(None, "ch", None),
        P(None, "ch"),
        P(None, "ch", None),
        P(None, "ch"),
        P("ch"),
        P("ch"),
    )
    return jax.shard_map(
        on_device, mesh=mesh, in_specs=placed, out_specs=P("ch", "sp", None), check_vma=False
    )
```

```python
import math

import jax
import jax.numpy as jnp
from jax import lax
from jax.experimental import pallas as pl
from jax.experimental.pallas import tpu as pltpu
from jax.sharding import PartitionSpec as P

F32 = jnp.float32
BF16 = jnp.bfloat16
LANES = 128
EXACT = lax.Precision.HIGHEST
NEG_LOG2E = -1.0 / math.log(2.0)

CHUNK = 8
X_ROWS = 3
BACK = 6
PROJ_PAIRS = 80
VEC_PAIRS = 32


def iota(shape, axis):
    return lax.broadcasted_iota(jnp.int32, shape, axis)


def spread(chans, offset):
    lane = iota((chans, 2 * chans), 1)
    return jnp.where(lane == 2 * iota((chans, 2 * chans), 0) + offset, 1.0, 0.0).astype(F32)


def dup_rows(value, dup):
    return jnp.dot(value, dup, preferred_element_type=F32, precision=EXACT)


def softplus(x):
    return jnp.maximum(x, 0.0) + jnp.log(1.0 + jnp.exp(-jnp.abs(x)))


def silu(x):
    return x * jax.nn.sigmoid(x)


def roll(x, shift, axis):
    return pltpu.roll(x, shift % x.shape[axis], axis)


def start_copies(sources, targets, arrived):
    copies = [
        pltpu.make_async_copy(source, target, arrived.at[index])
        for index, (source, target) in enumerate(zip(sources, targets))
    ]
    for copy in copies:
        copy.start()
    return copies


def prep_kernel(*refs):
    count, kept = 11, 7
    sources, send_ref, col_mask_ref, row_mask_ref = refs[:count], *refs[count : count + 3]
    handed = refs[count + 3 : count + 3 + kept]
    scr, tile, vec, near, packed, *own, arrived = refs[count + 3 + kept :]
    loaded = (*own, *handed)
    copies = start_copies(sources, loaded, arrived)
    for j in range(64):
        rows = slice(16 * j, 16 * j + 16)
        lane = iota((16, LANES), 1)
        col_mask_ref[rows, :] = jnp.where(lane[:, 0:64] == j, 1.0, 0.0).astype(BF16)
        row_mask_ref[rows, :] = jnp.where(lane // 2 == j, 1.0, 0.0).astype(BF16)
    for copy in copies[:8]:
        copy.wait()
    x_ref, cw_ref, cb_ref, pw_ref, dtw_ref, dtb_ref, rate_ref, skip_ref = loaded[:8]
    chans = cw_ref.shape[1]
    even, odd = spread(chans, 0), spread(chans, 1)
    even_b, odd_b = even.astype(BF16), odd.astype(BF16)
    half = VEC_PAIRS
    vec[0:9, :] = cw_ref[...]
    vec[9:10, :] = cb_ref[...]
    vec[10:12, :] = dtb_ref[2:4, :]
    vec[12:14, :] = skip_ref[2:4, :]
    vec[14:16, :] = jnp.zeros((2, chans), F32)
    vec[16:24, :] = dtw_ref[2]
    vec[24:32, :] = dtw_ref[3]
    vec[32:48, :] = rate_ref[2]
    vec[48:64, :] = rate_ref[3]
    high = vec[...].astype(BF16)
    low = (vec[0:half, :] - high[0:half].astype(F32)).astype(BF16)
    near[0:16, :] = rate_ref[0]
    near[16:24, :] = dtw_ref[0]
    near[24:25, :] = dtb_ref[0:1, :]
    near[25:26, :] = skip_ref[0:1, :] + skip_ref[1:2, :]
    near[26:32, :] = jnp.zeros((6, chans), F32)
    near[32:48, :] = rate_ref[1]
    near[48:56, :] = dtw_ref[1]
    near[56:57, :] = dtb_ref[1:2, :]
    near[57:64, :] = jnp.zeros((7, chans), F32)
    shared = near[...].astype(BF16)

    def pack(first, second):
        return jnp.dot(first, even_b, preferred_element_type=F32) + jnp.dot(
            second, odd_b, preferred_element_type=F32
        )

    parts = [pw_ref[k].astype(F32) for k in range(4)]
    first = [parts[k][0:8] for k in (2, 3, 0, 1)] + [parts[0][8:40], parts[1][8:24]]
    second = [parts[1][24:40], parts[2][8:40], parts[3][8:40]]
    packed[0:80, :] = pack(
        jnp.concatenate(first, axis=0).astype(BF16), jnp.concatenate(second, axis=0).astype(BF16)
    )
    packed[80:112, :] = pack(high[0:half], high[half:])
    packed[112:128, :] = pack(low[0:16], low[16:])
    packed[128:160, :] = pack(shared[0:half], shared[half:])

    turned = x_ref[...].astype(F32).T
    base = 2 * CHUNK
    scr[pl.ds(base + CHUNK, LANES, stride=CHUNK), :] = turned
    scr[pl.ds(base + 1, LANES, stride=CHUNK), :] = turned
    scr[pl.ds(base - CHUNK + 2, LANES, stride=CHUNK), :] = turned
    scr[base : base + 1, :] = jnp.zeros((1, LANES), F32)
    last = base + CHUNK * (LANES - 1) + 2
    scr[last : last + 1, :] = jnp.zeros((1, LANES), F32)
    slab = lax.axis_index("sp")
    for piece in range(CHUNK - X_ROWS):
        tile[X_ROWS + piece : X_ROWS + piece + 1, :] = packed[pl.ds(32 * piece + slab, 1), :]
    chunks = scr[base : base + CHUNK * LANES, :].reshape(LANES, CHUNK, LANES)
    is_x = iota((1, CHUNK, LANES), 1) < X_ROWS
    chunks = jnp.where(is_x, chunks, tile[...][None])
    send_ref[...] = chunks.reshape(CHUNK * LANES, LANES).astype(BF16)
    for copy in copies[8:]:
        copy.wait()


def lane_rows(parts, columns, mask_ref, weights):
    picked = [parts * mask_ref[16 * j : 16 * j + 16, :] for j in columns]
    return jnp.dot(jnp.concatenate(picked, axis=0), weights, preferred_element_type=F32)


def scan_pair(steps, rates, delta_ref, drive_ref, expand, wide_ref, part_ref, row_of):
    blocks = delta_ref.shape[1]
    states = [[jnp.zeros((16, LANES), F32) for _ in range(blocks)] for _ in range(2)]

    def prepare(turn):
        for way in range(2):
            first = 8 * turn if way == 0 else steps - 8 - 8 * turn
            for which in range(2):
                wide_ref[way, which, 16 * first : 16 * first + LANES, :] = expand(way, which, first)

    prepare(0)
    for step in range(steps):
        if step % 8 == 0 and step + 8 < steps:
            prepare(step // 8 + 1)
        for way in range(2):
            at = step if way == 0 else steps - 1 - step
            row = row_of(at)
            b_now, c_now = (wide_ref[way, which, 16 * at : 16 * at + 16, :] for which in range(2))
            for block in range(blocks):
                delta = delta_ref[way, block, row : row + 1, :]
                drive = drive_ref[way, block, row : row + 1, :]
                decay = jnp.exp2(delta * rates[way][block])
                state = decay * states[way][block] + drive * b_now
                states[way][block] = state
                product = c_now * state
                part_ref[way, block, 8 * row : 8 * row + 8, :] = product[0:8] + product[8:16]


def outputs_of(part_ref, block, half_ref):
    rows = part_ref.shape[2] // 8
    total = None
    for way in range(2):
        for lane_row in range(4):
            term = part_ref[way, block, pl.ds(lane_row, 2 * rows, stride=4), :]
            total = term if total is None else total + term
    half_ref[0 : 2 * rows, :] = total
    return half_ref[pl.ds(0, rows, stride=2), :] + half_ref[pl.ds(1, rows, stride=2), :]


def halves(value):
    high = value.astype(BF16)
    return high, (value - high.astype(F32)).astype(BF16)


def two_part_dot(value, high, low):
    return jnp.dot(value, high, preferred_element_type=F32) + jnp.dot(
        value, low, preferred_element_type=F32
    )


def row_weights(dtw_ref, dtb_ref, rate_ref, skip_ref, vec_ref, dup):
    for way in range(2):
        vec_ref[16 * way : 16 * way + 16, :] = dup_rows(rate_ref[way], dup) * NEG_LOG2E
        vec_ref[32 + 8 * way : 40 + 8 * way, :] = dup_rows(dtw_ref[way], dup)
    vec_ref[48:52, :] = dup_rows(dtb_ref[...], dup)
    skip = dup_rows(skip_ref[...], dup)
    vec_ref[52:53, :] = skip[0:1] + skip[1:2]
    vec_ref[53:56, :] = jnp.zeros((3, LANES), F32)


def step_weights(vec_refs):
    lane_row = iota((8, LANES), 1) % 2
    columns = []
    for ref in vec_refs:
        for way in range(2):
            dt_rows = ref[32 + 8 * way : 40 + 8 * way, :]
            column = []
            for row in range(2):
                column.append(jnp.zeros((16 + 8 * way, LANES), F32))
                column.append(jnp.where(lane_row == row, dt_rows, 0.0))
                column += [] if way else [jnp.zeros((8, LANES), F32)]
            columns.append(jnp.concatenate(column, axis=0))
    high, low = halves(jnp.concatenate(columns, axis=1))
    return jnp.concatenate([high, low], axis=0)


def column_kernel(
    recv_ref,
    mask_ref,
    dtw_ref,
    dtb_ref,
    rate_ref,
    skip_ref,
    gain_ref,
    bias_ref,
    gate_in_ref,
    send_ref,
    own_ref,
    near_ref,
    steps_ref,
    gate_ref,
    affine_ref,
    flat_scr,
    back_scr,
    scr,
    swap_scr,
    delta_scr,
    drive_scr,
    part_scr,
    half_scr,
    wide_scr,
):
    slabs = LANES // 4
    pad = 8
    flat_scr[...] = recv_ref[...].astype(F32)
    swapped = iota((LANES, LANES), 1) ^ 1
    for row in range(CHUNK):
        value = flat_scr[pl.ds(row, LANES, stride=CHUNK), :]
        scr[row] = value
        if row < X_ROWS:
            swap_scr[row, pad - 4 : pad, :] = jnp.zeros((4, LANES), F32)
            swap_scr[row, pad + LANES : pad + LANES + 4, :] = jnp.zeros((4, LANES), F32)
            swap_scr[row, pad : pad + LANES, :] = jnp.take_along_axis(
                value, swapped, axis=1, mode="promise_in_bounds"
            )

    even = iota((slabs, LANES), 1) % 2 == 0
    vecs = []
    projs = []
    conv = []
    for group in range(4):

        def rows_of(row):
            return scr[row, pl.ds(group, slabs, stride=4), :]

        def swapped_of(row, shift):
            return swap_scr[row, pl.ds(pad + group + 4 * shift, slabs, stride=4), :]

        pieces = [rows_of(row) for row in range(X_ROWS, CHUNK)]
        projs.append([pieces[0], pieces[1], pieces[2][0:16]])
        low = pieces[3][16:32]
        even_16 = even[0:16]
        vec = jnp.concatenate(
            [
                pieces[2][16:32] + jnp.where(even_16, low, 0.0),
                pieces[3][0:16] + jnp.where(even_16, roll(low, -1, 1), 0.0),
            ],
            axis=0,
        )
        vecs.append(vec)
        taps = jnp.where(even[0:16], vec[0:16], roll(vec[0:16], 1, 1))
        total = jnp.zeros((slabs, LANES), F32) + taps[9:10, :]
        for side in range(3):
            above, below = taps[side : side + 1, :], taps[6 + side : 7 + side, :]
            beyond = jnp.where(even, swapped_of(side, -1), swapped_of(side, 1))
            total = total + jnp.where(even[0:1], above, below) * beyond
            total = total + jnp.where(even[0:1], below, above) * swapped_of(side, 0)
            total = total + taps[3 + side : 4 + side, :] * rows_of(side)
        conv.append(silu(total).astype(BF16).astype(F32))

    shared = scr[CHUNK - 1, pl.ds(lax.axis_index("ch") ^ 2, slabs, stride=4), :]
    for way, value in enumerate(
        (jnp.where(even, shared, roll(shared, 1, 1)), jnp.where(even, roll(shared, -1, 1), shared))
    ):
        near_ref[16 * way : 16 * way + 16, :] = value[0:16] * NEG_LOG2E
        near_ref[32 + 8 * way : 40 + 8 * way, :] = value[16:24]
        near_ref[48 + way : 49 + way, :] = value[24:25]
        if way == 0:
            near_ref[52:53, :] = value[25:26]
    near_ref[50:52, :] = jnp.zeros((2, LANES), F32)
    near_ref[53:56, :] = jnp.zeros((3, LANES), F32)

    chans = dtw_ref.shape[2]
    dup = spread(chans, 0) + spread(chans, 1)
    row_weights(dtw_ref, dtb_ref, rate_ref, skip_ref, own_ref, dup)
    steps_ref[...] = step_weights((own_ref, near_ref))
    gate_ref[...] = silu(gate_in_ref[...].astype(F32))
    pick = iota((LANES, LANES), 0) == iota((LANES, LANES), 1)
    for index, ref in enumerate((gain_ref, bias_ref)):
        column = jnp.sum(jnp.where(pick, dup_rows(ref[...], dup), 0.0), axis=1, keepdims=True)
        affine_ref[index] = jnp.broadcast_to(column, (LANES, LANES))

    def from_even(left, right):
        mask = iota(left.shape, 1) % 2 == 0
        return jnp.where(mask, left, roll(right, 1, 1))

    def from_odd(left, right):
        mask = iota(left.shape, 1) % 2 == 0
        return jnp.where(mask, roll(left, -1, 1), right)

    def all_groups(take, parts):
        return jnp.concatenate([take(parts[0], parts[1]), take(parts[2], parts[3])], axis=1)

    values = jnp.concatenate([all_groups(from_even, conv), all_groups(from_odd, conv)], axis=0)
    values_b = values.astype(BF16)
    proj_w = jnp.concatenate(
        [
            all_groups(take, [p[piece] for p in projs])
            for take in (from_even, from_odd)
            for piece in range(3)
        ],
        axis=0,
    ).astype(BF16)
    vec = jnp.concatenate([all_groups(from_even, vecs), all_groups(from_odd, vecs)], axis=0)

    nt = (((1,), (1,)), ((), ()))
    proj = lax.dot_general(values_b, proj_w[0:128], nt, preferred_element_type=F32)
    proj = proj.astype(BF16)
    low = proj[:, 0:16]
    proj = proj.astype(F32)
    turned = lax.dot_general(proj_w[96:160], values_b, nt, preferred_element_type=F32)
    turned = turned.astype(BF16)

    dt_rows = vec[16:32]
    second_half = iota((16, 256), 0) >= 8
    rates = []
    for way in range(2):
        chosen = jnp.where(second_half == (way == 1), dt_rows, 0.0)
        delta = softplus(two_part_dot(low, *halves(chosen)) + vec[10 + way : 11 + way, :])
        drive = delta * values
        scaled = vec[32 + 16 * way : 48 + 16 * way] * NEG_LOG2E
        rates.append([scaled[:, 0:LANES], scaled[:, LANES:]])
        for block in range(2):
            lanes = slice(LANES * block, LANES * block + LANES)
            delta_scr[way, block] = delta[:, lanes]
            drive_scr[way, block] = drive[:, lanes]

    def row_of(at):
        return (at % 2) * slabs + at // 2

    ones = jnp.ones((64, LANES), BF16)

    def expand(way, which, first):
        parts = turned[32 * way + 16 * which : 32 * way + 16 * which + 16]
        return lane_rows(parts, [row_of(first + j) for j in range(8)], mask_ref, ones)

    scan_pair(2 * slabs, rates, delta_scr, drive_scr, expand, wide_scr, part_scr, row_of)

    skip = vec[12:13] + vec[13:14]
    backs = []
    for block in range(2):
        lanes = slice(LANES * block, LANES * block + LANES)
        y = outputs_of(part_scr, block, half_scr) + skip[:, lanes] * values[:, lanes]
        y_even, y_odd = y[0:slabs], y[slabs:]
        backs.append(jnp.where(even, y_even, roll(y_odd, 1, 1)))
        backs.append(jnp.where(even, roll(y_even, -1, 1), y_odd))
    for group in range(4):
        near = group ^ 2
        parts = (backs[group], conv[group], proj[0:slabs], proj[slabs:], backs[near], conv[near])
        for row, value in enumerate(parts):
            scr[row, pl.ds(group, slabs, stride=4), :] = value
    for row in range(BACK):
        back_scr[pl.ds(row, LANES, stride=BACK), :] = scr[row, 0:LANES, :]
    send_ref[...] = back_scr[...].astype(BF16)


def row_kernel(
    recv_ref,
    mask_ref,
    own_ref,
    near_ref,
    steps_ref,
    comb_ref,
    sums_ref,
    scr,
    mixed_scr,
    delta_scr,
    drive_scr,
    part_scr,
    half_scr,
    wide_scr,
):
    cols = LANES
    scr[...] = recv_ref[...].astype(F32)

    def chunk_row(row):
        return scr[pl.ds(row, cols, stride=BACK), :]

    proj = [chunk_row(2), chunk_row(3)]
    lane = iota((cols, LANES), 1)
    both = jnp.where(lane < 32, proj[0], roll(proj[1], 32, 1))
    both = both[:, 0:64].astype(BF16)
    low_rank = two_part_dot(both, steps_ref[0:64, :], steps_ref[64:, :])
    vecs = (own_ref, near_ref)
    verticals = (chunk_row(0), chunk_row(4))
    values = (chunk_row(1), chunk_row(5))
    for block in range(2):
        for way in range(2):
            first = LANES * (2 * block + way)
            delta = softplus(
                low_rank[:, first : first + LANES] + vecs[block][48 + way : 49 + way, :]
            )
            delta_scr[way, block] = delta
            drive_scr[way, block] = delta * values[block]
    rates = [[vec[16 * way : 16 * way + 16, :] for vec in vecs] for way in range(2)]

    for row in range(2):
        mixed_scr[pl.ds(row, cols, stride=2), :] = proj[row]
    turned = mixed_scr[...].T
    alike = iota((LANES, LANES), 0) % 2 == iota((LANES, LANES), 1) % 2
    by_row = jnp.where(alike, 1.0, 0.0).astype(BF16)

    def expand(way, which, first):
        top = 32 + 32 * way + 16 * which
        start = LANES * (first // 64)
        parts = turned[top : top + 16, start : start + LANES].astype(BF16)
        return lane_rows(parts, [(first + j) % 64 for j in range(8)], mask_ref, by_row)

    scan_pair(cols, rates, delta_scr, drive_scr, expand, wide_scr, part_scr, lambda at: at)
    sums = [jnp.zeros((8, LANES), F32) for _ in range(2)]
    for block in range(2):
        combined = (
            outputs_of(part_scr, block, half_scr)
            + vecs[block][52:53, :] * values[block]
            + verticals[block]
        )
        combined = combined.T
        if block == 0:
            comb_ref[...] = combined
        for tile in range(LANES // 8):
            rows = combined[8 * tile : 8 * tile + 8]
            sums = [sums[0] + rows, sums[1] + rows * rows]
    for index, value in enumerate(sums):
        value = value + roll(value, 4, 0)
        value = value + roll(value, 2, 0)
        sums_ref[8 * index : 8 * index + 8, :] = value


def norm_kernel(total_chans, comb_ref, s0_ref, s1_ref, gate_ref, affine_ref, out_ref):
    sums = s0_ref[...] + s1_ref[...]
    mean = sums[0:8] / total_chans
    var = sums[8:16] / total_chans - mean * mean
    scale = lax.rsqrt(var + 1e-05)
    comb = comb_ref[...]
    means = jnp.concatenate([mean] * (LANES // 8), axis=0)
    scales = jnp.concatenate([scale] * (LANES // 8), axis=0)
    normed = (comb - means) * scales * affine_ref[0] + affine_ref[1]
    out_ref[...] = (normed * gate_ref[...]).astype(BF16)


VMEM = pl.BlockSpec(memory_space=pltpu.VMEM)


def call(kernel, name, outs, scratch, inputs, place=VMEM, grant=24 << 20):
    single = not isinstance(outs, (list, tuple))
    return pl.pallas_call(
        kernel,
        out_shape=outs,
        in_specs=[place] * len(inputs),
        out_specs=VMEM if single else [VMEM] * len(outs),
        scratch_shapes=scratch,
        name=name,
        compiler_params=pltpu.CompilerParams(vmem_limit_bytes=grant),
    )(*inputs)


def other(value, flip):
    return lax.ppermute(value, "ch", [(i, i ^ flip) for i in range(lax.axis_size("ch"))])


def exchange(value, chunk, tile):
    peers = value.shape[0] // chunk
    pieces = value.reshape(peers, chunk // tile, tile, LANES)
    moved = lax.all_to_all(pieces, ("sp", "ch"), split_axis=0, concat_axis=0, tiled=True)
    return moved.reshape(value.shape)


def on_device(
    x_in,
    gate_in,
    conv_weight,
    conv_bias,
    proj_weight,
    dt_weight,
    dt_bias,
    decay_rate,
    skip_gain,
    norm_gain,
    norm_bias,
):
    chans, rows, cols = x_in.shape
    total_chans = chans * lax.axis_size("ch")
    flat = (chans * rows, cols)
    struct = jax.ShapeDtypeStruct

    def vm(*shape):
        return pltpu.VMEM(shape, F32)

    dt_weight = dt_weight.transpose(0, 2, 1)
    decay_rate = decay_rate.transpose(0, 2, 1)
    arguments = [
        pltpu.with_memory_space_constraint(value, pltpu.HBM)
        for value in (
            x_in.reshape(flat),
            conv_weight.T,
            conv_bias.reshape(1, chans),
            proj_weight,
            dt_weight,
            dt_bias,
            decay_rate,
            skip_gain,
            norm_gain.reshape(1, chans),
            norm_bias.reshape(1, chans),
            gate_in.reshape(flat),
        )
    ]
    send, col_mask, row_mask, *handed = call(
        prep_kernel,
        "prep",
        [
            struct((CHUNK * cols, LANES), BF16),
            struct((64 * 16, 64), BF16),
            struct((64 * 16, LANES), BF16),
        ]
        + [struct(value.shape, value.dtype) for value in arguments[4:]],
        [
            vm(CHUNK * (cols + 4), LANES),
            vm(CHUNK, LANES),
            vm(2 * VEC_PAIRS, chans),
            vm(64, chans),
            vm(160, LANES),
        ]
        + [pltpu.VMEM(value.shape, value.dtype) for value in arguments[:4]]
        + [pltpu.SemaphoreType.DMA((len(arguments),))],
        arguments,
        pl.BlockSpec(memory_space=pltpu.HBM),
    )
    send, own, near, steps, gate, affine = call(
        column_kernel,
        "columns",
        [
            struct((BACK * cols, LANES), BF16),
            struct((56, LANES), F32),
            struct((56, LANES), F32),
            struct((LANES, 4 * LANES), BF16),
            struct((LANES, cols), F32),
            struct((2, LANES, cols), F32),
        ],
        [
            vm(CHUNK * cols, LANES),
            vm(BACK * cols, LANES),
            vm(CHUNK, cols, LANES),
            vm(X_ROWS, cols + 16, LANES),
            vm(2, 2, 64, LANES),
            vm(2, 2, 64, LANES),
            vm(2, 2, 8 * 64, LANES),
            vm(LANES, LANES),
            vm(2, 2, 16 * 64, LANES),
        ],
        [exchange(send, CHUNK, CHUNK), col_mask] + handed,
    )
    received = exchange(send, BACK, 2)
    combined, sums = call(
        row_kernel,
        "rows",
        [struct((LANES, cols), F32), struct((16, cols), F32)],
        [
            vm(BACK * cols, LANES),
            vm(2 * cols, LANES),
            vm(2, 2, cols, LANES),
            vm(2, 2, cols, LANES),
            vm(2, 2, 8 * cols, LANES),
            vm(2 * cols, LANES),
            vm(2, 2, 16 * cols, LANES),
        ],
        [received, row_mask, own, near, steps],
    )
    out = call(
        lambda *refs: norm_kernel(total_chans, *refs),
        "norm",
        struct(flat, BF16),
        [],
        [combined, sums, other(sums, 1), gate, affine],
    )
    return out.reshape(chans, rows, cols)


def solution(mesh):
    placed = (
        P("ch", "sp", None),
        P("ch", "sp", None),
        P("ch", None),
        P("ch"),
        P(None, None, "ch"),
        P(None, "ch", None),
        P(None, "ch"),
        P(None, "ch", None),
        P(None, "ch"),
        P("ch"),
        P("ch"),
    )
    return jax.shard_map(
        on_device, mesh=mesh, in_specs=placed, out_specs=P("ch", "sp", None), check_vma=False
    )
```

```python
import math

import jax
import jax.numpy as jnp
from jax import lax
from jax.experimental import pallas as pl
from jax.experimental.pallas import tpu as pltpu
from jax.sharding import PartitionSpec as P

F32 = jnp.float32
BF16 = jnp.bfloat16
LANES = 128
EXACT = lax.Precision.HIGHEST
NEG_LOG2E = -1.0 / math.log(2.0)

CHUNK = 8
X_ROWS = 3
BACK = 6
PROJ_PAIRS = 80
VEC_PAIRS = 32


def iota(shape, axis):
    return lax.broadcasted_iota(jnp.int32, shape, axis)


def spread(chans, offset):
    lane = iota((chans, 2 * chans), 1)
    return jnp.where(lane == 2 * iota((chans, 2 * chans), 0) + offset, 1.0, 0.0).astype(F32)


def dup_rows(value, dup):
    return jnp.dot(value, dup, preferred_element_type=F32, precision=EXACT)


def softplus(x):
    return jnp.maximum(x, 0.0) + jnp.log(1.0 + jnp.exp(-jnp.abs(x)))


def silu(x):
    return x * jax.nn.sigmoid(x)


def roll(x, shift, axis):
    return pltpu.roll(x, shift % x.shape[axis], axis)


def start_copies(sources, targets, arrived):
    copies = [
        pltpu.make_async_copy(source, target, arrived.at[index])
        for index, (source, target) in enumerate(zip(sources, targets))
    ]
    for copy in copies:
        copy.start()
    return copies


def prep_kernel(*refs):
    count, kept = 11, 7
    sources, send_ref, col_mask_ref, row_mask_ref = refs[:count], *refs[count : count + 3]
    handed = refs[count + 3 : count + 3 + kept]
    scr, tile, vec, near, packed, *own, arrived = refs[count + 3 + kept :]
    loaded = (*own, *handed)
    copies = start_copies(sources, loaded, arrived)
    for j in range(64):
        rows = slice(16 * j, 16 * j + 16)
        lane = iota((16, LANES), 1)
        col_mask_ref[rows, :] = jnp.where(lane[:, 0:64] == j, 1.0, 0.0).astype(BF16)
        row_mask_ref[rows, :] = jnp.where(lane // 2 == j, 1.0, 0.0).astype(BF16)
    for copy in copies[:8]:
        copy.wait()
    x_ref, cw_ref, cb_ref, pw_ref, dtw_ref, dtb_ref, rate_ref, skip_ref = loaded[:8]
    chans = cw_ref.shape[1]
    even, odd = spread(chans, 0), spread(chans, 1)
    even_b, odd_b = even.astype(BF16), odd.astype(BF16)
    half = VEC_PAIRS
    vec[0:9, :] = cw_ref[...]
    vec[9:10, :] = cb_ref[...]
    vec[10:12, :] = dtb_ref[2:4, :]
    vec[12:14, :] = skip_ref[2:4, :]
    vec[14:16, :] = jnp.zeros((2, chans), F32)
    vec[16:24, :] = dtw_ref[2]
    vec[24:32, :] = dtw_ref[3]
    vec[32:48, :] = rate_ref[2]
    vec[48:64, :] = rate_ref[3]
    high = vec[...].astype(BF16)
    low = (vec[0:half, :] - high[0:half].astype(F32)).astype(BF16)
    near[0:16, :] = rate_ref[0]
    near[16:24, :] = dtw_ref[0]
    near[24:25, :] = dtb_ref[0:1, :]
    near[25:26, :] = skip_ref[0:1, :] + skip_ref[1:2, :]
    near[26:32, :] = jnp.zeros((6, chans), F32)
    near[32:48, :] = rate_ref[1]
    near[48:56, :] = dtw_ref[1]
    near[56:57, :] = dtb_ref[1:2, :]
    near[57:64, :] = jnp.zeros((7, chans), F32)
    shared = near[...].astype(BF16)

    def pack(first, second):
        return jnp.dot(first, even_b, preferred_element_type=F32) + jnp.dot(
            second, odd_b, preferred_element_type=F32
        )

    parts = [pw_ref[k].astype(F32) for k in range(4)]
    first = [parts[k][0:8] for k in (2, 3, 0, 1)] + [parts[0][8:40], parts[1][8:24]]
    second = [parts[1][24:40], parts[2][8:40], parts[3][8:40]]
    packed[0:80, :] = pack(
        jnp.concatenate(first, axis=0).astype(BF16), jnp.concatenate(second, axis=0).astype(BF16)
    )
    packed[80:112, :] = pack(high[0:half], high[half:])
    packed[112:128, :] = pack(low[0:16], low[16:])
    packed[128:160, :] = pack(shared[0:half], shared[half:])

    turned = x_ref[...].astype(F32).T
    base = 2 * CHUNK
    scr[pl.ds(base + CHUNK, LANES, stride=CHUNK), :] = turned
    scr[pl.ds(base + 1, LANES, stride=CHUNK), :] = turned
    scr[pl.ds(base - CHUNK + 2, LANES, stride=CHUNK), :] = turned
    scr[base : base + 1, :] = jnp.zeros((1, LANES), F32)
    last = base + CHUNK * (LANES - 1) + 2
    scr[last : last + 1, :] = jnp.zeros((1, LANES), F32)
    slab = lax.axis_index("sp")
    for piece in range(CHUNK - X_ROWS):
        tile[X_ROWS + piece : X_ROWS + piece + 1, :] = packed[pl.ds(32 * piece + slab, 1), :]
    chunks = scr[base : base + CHUNK * LANES, :].reshape(LANES, CHUNK, LANES)
    is_x = iota((1, CHUNK, LANES), 1) < X_ROWS
    chunks = jnp.where(is_x, chunks, tile[...][None])
    send_ref[...] = chunks.reshape(CHUNK * LANES, LANES).astype(BF16)
    for copy in copies[8:]:
        copy.wait()


def lane_rows(parts, columns, mask_ref, weights):
    picked = [parts * mask_ref[16 * j : 16 * j + 16, :] for j in columns]
    return jnp.dot(jnp.concatenate(picked, axis=0), weights, preferred_element_type=F32)


def scan_pair(steps, rates, delta_ref, drive_ref, expand, wide_ref, part_ref, row_of):
    blocks = delta_ref.shape[1]
    states = [[jnp.zeros((16, LANES), F32) for _ in range(blocks)] for _ in range(2)]

    def prepare(turn):
        for way in range(2):
            first = 8 * turn if way == 0 else steps - 8 - 8 * turn
            for which in range(2):
                wide_ref[way, which, 16 * first : 16 * first + LANES, :] = expand(way, which, first)

    prepare(0)
    for step in range(steps):
        if step % 8 == 0 and step + 8 < steps:
            prepare(step // 8 + 1)
        for way in range(2):
            at = step if way == 0 else steps - 1 - step
            row = row_of(at)
            b_now, c_now = (wide_ref[way, which, 16 * at : 16 * at + 16, :] for which in range(2))
            for block in range(blocks):
                delta = delta_ref[way, block, row : row + 1, :]
                drive = drive_ref[way, block, row : row + 1, :]
                decay = jnp.exp2(delta * rates[way][block])
                state = decay * states[way][block] + drive * b_now
                states[way][block] = state
                product = c_now * state
                part_ref[way, block, 8 * row : 8 * row + 8, :] = product[0:8] + product[8:16]


def outputs_of(part_ref, block, half_ref):
    rows = part_ref.shape[2] // 8
    total = None
    for way in range(2):
        for lane_row in range(4):
            term = part_ref[way, block, pl.ds(lane_row, 2 * rows, stride=4), :]
            total = term if total is None else total + term
    half_ref[0 : 2 * rows, :] = total
    return half_ref[pl.ds(0, rows, stride=2), :] + half_ref[pl.ds(1, rows, stride=2), :]


def halves(value):
    high = value.astype(BF16)
    return high, (value - high.astype(F32)).astype(BF16)


def two_part_dot(value, high, low):
    return jnp.dot(value, high, preferred_element_type=F32) + jnp.dot(
        value, low, preferred_element_type=F32
    )


def row_weights(dtw_ref, dtb_ref, rate_ref, skip_ref, vec_ref, dup):
    for way in range(2):
        vec_ref[16 * way : 16 * way + 16, :] = dup_rows(rate_ref[way], dup) * NEG_LOG2E
        vec_ref[32 + 8 * way : 40 + 8 * way, :] = dup_rows(dtw_ref[way], dup)
    vec_ref[48:52, :] = dup_rows(dtb_ref[...], dup)
    skip = dup_rows(skip_ref[...], dup)
    vec_ref[52:53, :] = skip[0:1] + skip[1:2]
    vec_ref[53:56, :] = jnp.zeros((3, LANES), F32)


def step_weights(vec_refs):
    lane_row = iota((8, LANES), 1) % 2
    columns = []
    for ref in vec_refs:
        for way in range(2):
            dt_rows = ref[32 + 8 * way : 40 + 8 * way, :]
            column = []
            for row in range(2):
                column.append(jnp.zeros((16 + 8 * way, LANES), F32))
                column.append(jnp.where(lane_row == row, dt_rows, 0.0))
                column += [] if way else [jnp.zeros((8, LANES), F32)]
            columns.append(jnp.concatenate(column, axis=0))
    high, low = halves(jnp.concatenate(columns, axis=1))
    return jnp.concatenate([high, low], axis=0)


def column_kernel(
    recv_ref,
    mask_ref,
    dtw_ref,
    dtb_ref,
    rate_ref,
    skip_ref,
    send_ref,
    own_ref,
    near_ref,
    steps_ref,
    flat_scr,
    back_scr,
    scr,
    swap_scr,
    delta_scr,
    drive_scr,
    part_scr,
    half_scr,
    wide_scr,
):
    slabs = LANES // 4
    pad = 8
    flat_scr[...] = recv_ref[...].astype(F32)
    swapped = iota((LANES, LANES), 1) ^ 1
    for row in range(CHUNK):
        value = flat_scr[pl.ds(row, LANES, stride=CHUNK), :]
        scr[row] = value
        if row < X_ROWS:
            swap_scr[row, pad - 4 : pad, :] = jnp.zeros((4, LANES), F32)
            swap_scr[row, pad + LANES : pad + LANES + 4, :] = jnp.zeros((4, LANES), F32)
            swap_scr[row, pad : pad + LANES, :] = jnp.take_along_axis(
                value, swapped, axis=1, mode="promise_in_bounds"
            )

    even = iota((slabs, LANES), 1) % 2 == 0
    vecs = []
    projs = []
    conv = []
    for group in range(4):

        def rows_of(row):
            return scr[row, pl.ds(group, slabs, stride=4), :]

        def swapped_of(row, shift):
            return swap_scr[row, pl.ds(pad + group + 4 * shift, slabs, stride=4), :]

        pieces = [rows_of(row) for row in range(X_ROWS, CHUNK)]
        projs.append([pieces[0], pieces[1], pieces[2][0:16]])
        low = pieces[3][16:32]
        even_16 = even[0:16]
        vec = jnp.concatenate(
            [
                pieces[2][16:32] + jnp.where(even_16, low, 0.0),
                pieces[3][0:16] + jnp.where(even_16, roll(low, -1, 1), 0.0),
            ],
            axis=0,
        )
        vecs.append(vec)
        taps = jnp.where(even[0:16], vec[0:16], roll(vec[0:16], 1, 1))
        total = jnp.zeros((slabs, LANES), F32) + taps[9:10, :]
        for side in range(3):
            above, below = taps[side : side + 1, :], taps[6 + side : 7 + side, :]
            beyond = jnp.where(even, swapped_of(side, -1), swapped_of(side, 1))
            total = total + jnp.where(even[0:1], above, below) * beyond
            total = total + jnp.where(even[0:1], below, above) * swapped_of(side, 0)
            total = total + taps[3 + side : 4 + side, :] * rows_of(side)
        conv.append(silu(total).astype(BF16).astype(F32))

    shared = scr[CHUNK - 1, pl.ds(lax.axis_index("ch") ^ 2, slabs, stride=4), :]
    for way, value in enumerate(
        (jnp.where(even, shared, roll(shared, 1, 1)), jnp.where(even, roll(shared, -1, 1), shared))
    ):
        near_ref[16 * way : 16 * way + 16, :] = value[0:16] * NEG_LOG2E
        near_ref[32 + 8 * way : 40 + 8 * way, :] = value[16:24]
        near_ref[48 + way : 49 + way, :] = value[24:25]
        if way == 0:
            near_ref[52:53, :] = value[25:26]
    near_ref[50:52, :] = jnp.zeros((2, LANES), F32)
    near_ref[53:56, :] = jnp.zeros((3, LANES), F32)

    chans = dtw_ref.shape[2]
    dup = spread(chans, 0) + spread(chans, 1)
    row_weights(dtw_ref, dtb_ref, rate_ref, skip_ref, own_ref, dup)
    steps_ref[...] = step_weights((own_ref, near_ref))

    def from_even(left, right):
        mask = iota(left.shape, 1) % 2 == 0
        return jnp.where(mask, left, roll(right, 1, 1))

    def from_odd(left, right):
        mask = iota(left.shape, 1) % 2 == 0
        return jnp.where(mask, roll(left, -1, 1), right)

    def all_groups(take, parts):
        return jnp.concatenate([take(parts[0], parts[1]), take(parts[2], parts[3])], axis=1)

    values = jnp.concatenate([all_groups(from_even, conv), all_groups(from_odd, conv)], axis=0)
    values_b = values.astype(BF16)
    proj_w = jnp.concatenate(
        [
            all_groups(take, [p[piece] for p in projs])
            for take in (from_even, from_odd)
            for piece in range(3)
        ],
        axis=0,
    ).astype(BF16)
    vec = jnp.concatenate([all_groups(from_even, vecs), all_groups(from_odd, vecs)], axis=0)

    nt = (((1,), (1,)), ((), ()))
    proj = lax.dot_general(values_b, proj_w[0:128], nt, preferred_element_type=F32)
    proj = proj.astype(BF16)
    low = proj[:, 0:16]
    proj = proj.astype(F32)
    turned = lax.dot_general(proj_w[96:160], values_b, nt, preferred_element_type=F32)
    turned = turned.astype(BF16)

    dt_rows = vec[16:32]
    second_half = iota((16, 256), 0) >= 8
    rates = []
    for way in range(2):
        chosen = jnp.where(second_half == (way == 1), dt_rows, 0.0)
        delta = softplus(two_part_dot(low, *halves(chosen)) + vec[10 + way : 11 + way, :])
        drive = delta * values
        scaled = vec[32 + 16 * way : 48 + 16 * way] * NEG_LOG2E
        rates.append([scaled[:, 0:LANES], scaled[:, LANES:]])
        for block in range(2):
            lanes = slice(LANES * block, LANES * block + LANES)
            delta_scr[way, block] = delta[:, lanes]
            drive_scr[way, block] = drive[:, lanes]

    def row_of(at):
        return (at % 2) * slabs + at // 2

    ones = jnp.ones((64, LANES), BF16)

    def expand(way, which, first):
        parts = turned[32 * way + 16 * which : 32 * way + 16 * which + 16]
        return lane_rows(parts, [row_of(first + j) for j in range(8)], mask_ref, ones)

    scan_pair(2 * slabs, rates, delta_scr, drive_scr, expand, wide_scr, part_scr, row_of)

    skip = vec[12:13] + vec[13:14]
    backs = []
    for block in range(2):
        lanes = slice(LANES * block, LANES * block + LANES)
        y = outputs_of(part_scr, block, half_scr) + skip[:, lanes] * values[:, lanes]
        y_even, y_odd = y[0:slabs], y[slabs:]
        backs.append(jnp.where(even, y_even, roll(y_odd, 1, 1)))
        backs.append(jnp.where(even, roll(y_even, -1, 1), y_odd))
    for group in range(4):
        near = group ^ 2
        parts = (backs[group], conv[group], proj[0:slabs], proj[slabs:], backs[near], conv[near])
        for row, value in enumerate(parts):
            scr[row, pl.ds(group, slabs, stride=4), :] = value
    for row in range(BACK):
        back_scr[pl.ds(row, LANES, stride=BACK), :] = scr[row, 0:LANES, :]
    send_ref[...] = back_scr[...].astype(BF16)


def row_kernel(
    recv_ref,
    mask_ref,
    own_ref,
    near_ref,
    steps_ref,
    comb_ref,
    sums_ref,
    scr,
    mixed_scr,
    delta_scr,
    drive_scr,
    part_scr,
    half_scr,
    wide_scr,
):
    cols = LANES
    scr[...] = recv_ref[...].astype(F32)

    def chunk_row(row):
        return scr[pl.ds(row, cols, stride=BACK), :]

    proj = [chunk_row(2), chunk_row(3)]
    lane = iota((cols, LANES), 1)
    both = jnp.where(lane < 32, proj[0], roll(proj[1], 32, 1))
    both = both[:, 0:64].astype(BF16)
    low_rank = two_part_dot(both, steps_ref[0:64, :], steps_ref[64:, :])
    vecs = (own_ref, near_ref)
    verticals = (chunk_row(0), chunk_row(4))
    values = (chunk_row(1), chunk_row(5))
    for block in range(2):
        for way in range(2):
            first = LANES * (2 * block + way)
            delta = softplus(
                low_rank[:, first : first + LANES] + vecs[block][48 + way : 49 + way, :]
            )
            delta_scr[way, block] = delta
            drive_scr[way, block] = delta * values[block]
    rates = [[vec[16 * way : 16 * way + 16, :] for vec in vecs] for way in range(2)]

    for row in range(2):
        mixed_scr[pl.ds(row, cols, stride=2), :] = proj[row]
    turned = mixed_scr[...].T
    alike = iota((LANES, LANES), 0) % 2 == iota((LANES, LANES), 1) % 2
    by_row = jnp.where(alike, 1.0, 0.0).astype(BF16)

    def expand(way, which, first):
        top = 32 + 32 * way + 16 * which
        start = LANES * (first // 64)
        parts = turned[top : top + 16, start : start + LANES].astype(BF16)
        return lane_rows(parts, [(first + j) % 64 for j in range(8)], mask_ref, by_row)

    scan_pair(cols, rates, delta_scr, drive_scr, expand, wide_scr, part_scr, lambda at: at)
    sums = [jnp.zeros((8, LANES), F32) for _ in range(2)]
    for block in range(2):
        combined = (
            outputs_of(part_scr, block, half_scr)
            + vecs[block][52:53, :] * values[block]
            + verticals[block]
        )
        combined = combined.T
        if block == 0:
            comb_ref[...] = combined
        for tile in range(LANES // 8):
            rows = combined[8 * tile : 8 * tile + 8]
            sums = [sums[0] + rows, sums[1] + rows * rows]
    for index, value in enumerate(sums):
        value = value + roll(value, 4, 0)
        value = value + roll(value, 2, 0)
        sums_ref[8 * index : 8 * index + 8, :] = value


def gate_kernel(sums_ref, gain_ref, bias_ref, gate_in_ref, affine_ref):
    chans = gain_ref.shape[1]
    gate = silu(gate_in_ref[...].astype(F32))
    pick = iota((LANES, chans), 0) // 2 == iota((LANES, chans), 1)
    for index, ref in enumerate((gain_ref, bias_ref)):
        column = jnp.sum(jnp.where(pick, ref[...], 0.0), axis=1, keepdims=True)
        affine_ref[index] = column * gate


def norm_kernel(total_chans, comb_ref, s0_ref, s1_ref, affine_ref, out_ref):
    sums = s0_ref[...] + s1_ref[...]
    mean = sums[0:8] / total_chans
    var = sums[8:16] / total_chans - mean * mean
    scale = lax.rsqrt(var + 1e-05)
    comb = comb_ref[...]
    means = jnp.concatenate([mean] * (LANES // 8), axis=0)
    scales = jnp.concatenate([scale] * (LANES // 8), axis=0)
    out_ref[...] = ((comb - means) * scales * affine_ref[0] + affine_ref[1]).astype(BF16)


VMEM = pl.BlockSpec(memory_space=pltpu.VMEM)


def call(kernel, name, outs, scratch, inputs, place=VMEM, grant=24 << 20):
    single = not isinstance(outs, (list, tuple))
    return pl.pallas_call(
        kernel,
        out_shape=outs,
        in_specs=[place] * len(inputs),
        out_specs=VMEM if single else [VMEM] * len(outs),
        scratch_shapes=scratch,
        name=name,
        compiler_params=pltpu.CompilerParams(vmem_limit_bytes=grant),
    )(*inputs)


def other(value, flip):
    return lax.ppermute(value, "ch", [(i, i ^ flip) for i in range(lax.axis_size("ch"))])


def exchange(value, chunk, tile):
    peers = value.shape[0] // chunk
    pieces = value.reshape(peers, chunk // tile, tile, LANES)
    moved = lax.all_to_all(pieces, ("sp", "ch"), split_axis=0, concat_axis=0, tiled=True)
    return moved.reshape(value.shape)


def on_device(
    x_in,
    gate_in,
    conv_weight,
    conv_bias,
    proj_weight,
    dt_weight,
    dt_bias,
    decay_rate,
    skip_gain,
    norm_gain,
    norm_bias,
):
    chans, rows, cols = x_in.shape
    total_chans = chans * lax.axis_size("ch")
    flat = (chans * rows, cols)
    struct = jax.ShapeDtypeStruct

    def vm(*shape):
        return pltpu.VMEM(shape, F32)

    dt_weight = dt_weight.transpose(0, 2, 1)
    decay_rate = decay_rate.transpose(0, 2, 1)
    arguments = [
        pltpu.with_memory_space_constraint(value, pltpu.HBM)
        for value in (
            x_in.reshape(flat),
            conv_weight.T,
            conv_bias.reshape(1, chans),
            proj_weight,
            dt_weight,
            dt_bias,
            decay_rate,
            skip_gain,
            norm_gain.reshape(1, chans),
            norm_bias.reshape(1, chans),
            gate_in.reshape(flat),
        )
    ]
    send, col_mask, row_mask, *handed = call(
        prep_kernel,
        "prep",
        [
            struct((CHUNK * cols, LANES), BF16),
            struct((64 * 16, 64), BF16),
            struct((64 * 16, LANES), BF16),
        ]
        + [struct(value.shape, value.dtype) for value in arguments[4:]],
        [
            vm(CHUNK * (cols + 4), LANES),
            vm(CHUNK, LANES),
            vm(2 * VEC_PAIRS, chans),
            vm(64, chans),
            vm(160, LANES),
        ]
        + [pltpu.VMEM(value.shape, value.dtype) for value in arguments[:4]]
        + [pltpu.SemaphoreType.DMA((len(arguments),))],
        arguments,
        pl.BlockSpec(memory_space=pltpu.HBM),
    )
    send, own, near, steps = call(
        column_kernel,
        "columns",
        [
            struct((BACK * cols, LANES), BF16),
            struct((56, LANES), F32),
            struct((56, LANES), F32),
            struct((LANES, 4 * LANES), BF16),
        ],
        [
            vm(CHUNK * cols, LANES),
            vm(BACK * cols, LANES),
            vm(CHUNK, cols, LANES),
            vm(X_ROWS, cols + 16, LANES),
            vm(2, 2, 64, LANES),
            vm(2, 2, 64, LANES),
            vm(2, 2, 8 * 64, LANES),
            vm(LANES, LANES),
            vm(2, 2, 16 * 64, LANES),
        ],
        [exchange(send, CHUNK, CHUNK), col_mask] + handed[:4],
    )
    received = exchange(send, BACK, 2)
    combined, sums = call(
        row_kernel,
        "rows",
        [struct((LANES, cols), F32), struct((16, cols), F32)],
        [
            vm(BACK * cols, LANES),
            vm(2 * cols, LANES),
            vm(2, 2, cols, LANES),
            vm(2, 2, cols, LANES),
            vm(2, 2, 8 * cols, LANES),
            vm(2 * cols, LANES),
            vm(2, 2, 16 * cols, LANES),
        ],
        [received, row_mask, own, near, steps],
    )
    affine = call(
        gate_kernel, "gate", struct((2, LANES, cols), F32), [], [sums] + handed[4:]
    )
    out = call(
        lambda *refs: norm_kernel(total_chans, *refs),
        "norm",
        struct(flat, BF16),
        [],
        [combined, sums, other(sums, 1), affine],
    )
    return out.reshape(chans, rows, cols)


def solution(mesh):
    placed = (
        P("ch", "sp", None),
        P("ch", "sp", None),
        P("ch", None),
        P("ch"),
        P(None, None, "ch"),
        P(None, "ch", None),
        P(None, "ch"),
        P(None, "ch", None),
        P(None, "ch"),
        P("ch"),
        P("ch"),
    )
    return jax.shard_map(
        on_device, mesh=mesh, in_specs=placed, out_specs=P("ch", "sp", None), check_vma=False
    )
```

```python
import math

import jax
import jax.numpy as jnp
from jax import lax
from jax.experimental import pallas as pl
from jax.experimental.pallas import tpu as pltpu
from jax.sharding import PartitionSpec as P

F32 = jnp.float32
BF16 = jnp.bfloat16
LANES = 128
EXACT = lax.Precision.HIGHEST
NEG_LOG2E = -1.0 / math.log(2.0)

CHUNK = 8
X_ROWS = 3
BACK = 6
PROJ_PAIRS = 80
VEC_PAIRS = 32


def iota(shape, axis):
    return lax.broadcasted_iota(jnp.int32, shape, axis)


def spread(chans, offset):
    lane = iota((chans, 2 * chans), 1)
    return jnp.where(lane == 2 * iota((chans, 2 * chans), 0) + offset, 1.0, 0.0).astype(F32)


def dup_rows(value, dup):
    return jnp.dot(value, dup, preferred_element_type=F32, precision=EXACT)


def softplus(x):
    return jnp.maximum(x, 0.0) + jnp.log(1.0 + jnp.exp(-jnp.abs(x)))


def silu(x):
    return x * jax.nn.sigmoid(x)


def roll(x, shift, axis):
    return pltpu.roll(x, shift % x.shape[axis], axis)


def start_copies(sources, targets, arrived):
    copies = [
        pltpu.make_async_copy(source, target, arrived.at[index])
        for index, (source, target) in enumerate(zip(sources, targets))
    ]
    for copy in copies:
        copy.start()
    return copies


def prep_kernel(*refs):
    count, kept = 11, 7
    sources, send_ref, col_mask_ref, row_mask_ref = refs[:count], *refs[count : count + 3]
    handed = refs[count + 3 : count + 3 + kept]
    scr, tile, vec, near, packed, *own, arrived = refs[count + 3 + kept :]
    loaded = (*own, *handed)
    copies = start_copies(sources, loaded, arrived)
    for j in range(64):
        rows = slice(16 * j, 16 * j + 16)
        lane = iota((16, LANES), 1)
        col_mask_ref[rows, :] = jnp.where(lane[:, 0:64] == j, 1.0, 0.0).astype(BF16)
        row_mask_ref[rows, :] = jnp.where(lane // 2 == j, 1.0, 0.0).astype(BF16)
    for copy in copies[:8]:
        copy.wait()
    x_ref, cw_ref, cb_ref, pw_ref, dtw_ref, dtb_ref, rate_ref, skip_ref = loaded[:8]
    chans = cw_ref.shape[1]
    even, odd = spread(chans, 0), spread(chans, 1)
    even_b, odd_b = even.astype(BF16), odd.astype(BF16)
    half = VEC_PAIRS
    vec[0:9, :] = cw_ref[...]
    vec[9:10, :] = cb_ref[...]
    vec[10:12, :] = dtb_ref[2:4, :]
    vec[12:14, :] = skip_ref[2:4, :]
    vec[14:16, :] = jnp.zeros((2, chans), F32)
    vec[16:24, :] = dtw_ref[2]
    vec[24:32, :] = dtw_ref[3]
    vec[32:48, :] = rate_ref[2]
    vec[48:64, :] = rate_ref[3]
    high = vec[...].astype(BF16)
    low = (vec[0:half, :] - high[0:half].astype(F32)).astype(BF16)
    near[0:16, :] = rate_ref[0]
    near[16:24, :] = dtw_ref[0]
    near[24:25, :] = dtb_ref[0:1, :]
    near[25:26, :] = skip_ref[0:1, :] + skip_ref[1:2, :]
    near[26:32, :] = jnp.zeros((6, chans), F32)
    near[32:48, :] = rate_ref[1]
    near[48:56, :] = dtw_ref[1]
    near[56:57, :] = dtb_ref[1:2, :]
    near[57:64, :] = jnp.zeros((7, chans), F32)
    shared = near[...].astype(BF16)

    def pack(first, second):
        return jnp.dot(first, even_b, preferred_element_type=F32) + jnp.dot(
            second, odd_b, preferred_element_type=F32
        )

    parts = [pw_ref[k].astype(F32) for k in range(4)]
    first = [parts[k][0:8] for k in (2, 3, 0, 1)] + [parts[0][8:40], parts[1][8:24]]
    second = [parts[1][24:40], parts[2][8:40], parts[3][8:40]]
    packed[0:80, :] = pack(
        jnp.concatenate(first, axis=0).astype(BF16), jnp.concatenate(second, axis=0).astype(BF16)
    )
    packed[80:112, :] = pack(high[0:half], high[half:])
    packed[112:128, :] = pack(low[0:16], low[16:])
    packed[128:160, :] = pack(shared[0:half], shared[half:])

    turned = x_ref[...].astype(F32).T
    base = 2 * CHUNK
    scr[pl.ds(base + CHUNK, LANES, stride=CHUNK), :] = turned
    scr[pl.ds(base + 1, LANES, stride=CHUNK), :] = turned
    scr[pl.ds(base - CHUNK + 2, LANES, stride=CHUNK), :] = turned
    scr[base : base + 1, :] = jnp.zeros((1, LANES), F32)
    last = base + CHUNK * (LANES - 1) + 2
    scr[last : last + 1, :] = jnp.zeros((1, LANES), F32)
    slab = lax.axis_index("sp")
    for piece in range(CHUNK - X_ROWS):
        tile[X_ROWS + piece : X_ROWS + piece + 1, :] = packed[pl.ds(32 * piece + slab, 1), :]
    chunks = scr[base : base + CHUNK * LANES, :].reshape(LANES, CHUNK, LANES)
    is_x = iota((1, CHUNK, LANES), 1) < X_ROWS
    chunks = jnp.where(is_x, chunks, tile[...][None])
    send_ref[...] = chunks.reshape(CHUNK * LANES, LANES).astype(BF16)
    for copy in copies[8:]:
        copy.wait()


def lane_rows(pieces, columns, mask_ref, weights):
    picked = [parts * mask_ref[16 * j : 16 * j + 16, :] for parts in pieces for j in columns]
    wide = jnp.dot(jnp.concatenate(picked, axis=0), weights, preferred_element_type=F32)
    return wide.reshape(len(pieces), LANES, LANES)


def scan_pair(steps, rates, delta_ref, drive_ref, expand, wide_ref, part_ref, row_of):
    blocks = delta_ref.shape[1]
    states = [[jnp.zeros((16, LANES), F32) for _ in range(blocks)] for _ in range(2)]

    def prepare(turn):
        for way in range(2):
            first = 8 * turn if way == 0 else steps - 8 - 8 * turn
            wide = expand(way, first)
            for which in range(2):
                wide_ref[way, which, 16 * first : 16 * first + LANES, :] = wide[which]

    prepare(0)
    for step in range(steps):
        if step % 8 == 0 and step + 8 < steps:
            prepare(step // 8 + 1)
        for way in range(2):
            at = step if way == 0 else steps - 1 - step
            row = row_of(at)
            b_now, c_now = (wide_ref[way, which, 16 * at : 16 * at + 16, :] for which in range(2))
            for block in range(blocks):
                delta = delta_ref[way, block, row : row + 1, :]
                drive = drive_ref[way, block, row : row + 1, :]
                decay = jnp.exp2(delta * rates[way][block])
                state = decay * states[way][block] + drive * b_now
                states[way][block] = state
                product = c_now * state
                part_ref[way, block, 8 * row : 8 * row + 8, :] = product[0:8] + product[8:16]


def outputs_of(part_ref, block, half_ref):
    rows = part_ref.shape[2] // 8
    total = None
    for way in range(2):
        for lane_row in range(4):
            term = part_ref[way, block, pl.ds(lane_row, 2 * rows, stride=4), :]
            total = term if total is None else total + term
    half_ref[0 : 2 * rows, :] = total
    return half_ref[pl.ds(0, rows, stride=2), :] + half_ref[pl.ds(1, rows, stride=2), :]


def halves(value):
    high = value.astype(BF16)
    return high, (value - high.astype(F32)).astype(BF16)


def two_part_dot(value, high, low):
    return jnp.dot(value, high, preferred_element_type=F32) + jnp.dot(
        value, low, preferred_element_type=F32
    )


def row_weights(dtw_ref, dtb_ref, rate_ref, skip_ref, vec_ref, dup):
    for way in range(2):
        vec_ref[16 * way : 16 * way + 16, :] = dup_rows(rate_ref[way], dup) * NEG_LOG2E
        vec_ref[32 + 8 * way : 40 + 8 * way, :] = dup_rows(dtw_ref[way], dup)
    vec_ref[48:52, :] = dup_rows(dtb_ref[...], dup)
    skip = dup_rows(skip_ref[...], dup)
    vec_ref[52:53, :] = skip[0:1] + skip[1:2]
    vec_ref[53:56, :] = jnp.zeros((3, LANES), F32)


def step_weights(vec_refs):
    lane_row = iota((8, LANES), 1) % 2
    columns = []
    for ref in vec_refs:
        for way in range(2):
            dt_rows = ref[32 + 8 * way : 40 + 8 * way, :]
            column = []
            for row in range(2):
                column.append(jnp.zeros((16 + 8 * way, LANES), F32))
                column.append(jnp.where(lane_row == row, dt_rows, 0.0))
                column += [] if way else [jnp.zeros((8, LANES), F32)]
            columns.append(jnp.concatenate(column, axis=0))
    high, low = halves(jnp.concatenate(columns, axis=1))
    return jnp.concatenate([high, low], axis=0)


def column_kernel(
    recv_ref,
    mask_ref,
    dtw_ref,
    dtb_ref,
    rate_ref,
    skip_ref,
    send_ref,
    own_ref,
    near_ref,
    steps_ref,
    flat_scr,
    back_scr,
    scr,
    swap_scr,
    delta_scr,
    drive_scr,
    part_scr,
    half_scr,
    wide_scr,
):
    slabs = LANES // 4
    pad = 8
    flat_scr[...] = recv_ref[...].astype(F32)
    swapped = iota((LANES, LANES), 1) ^ 1
    for row in range(CHUNK):
        value = flat_scr[pl.ds(row, LANES, stride=CHUNK), :]
        scr[row] = value
        if row < X_ROWS:
            swap_scr[row, pad - 4 : pad, :] = jnp.zeros((4, LANES), F32)
            swap_scr[row, pad + LANES : pad + LANES + 4, :] = jnp.zeros((4, LANES), F32)
            swap_scr[row, pad : pad + LANES, :] = jnp.take_along_axis(
                value, swapped, axis=1, mode="promise_in_bounds"
            )

    even = iota((slabs, LANES), 1) % 2 == 0
    vecs = []
    projs = []
    conv = []
    for group in range(4):

        def rows_of(row):
            return scr[row, pl.ds(group, slabs, stride=4), :]

        def swapped_of(row, shift):
            return swap_scr[row, pl.ds(pad + group + 4 * shift, slabs, stride=4), :]

        pieces = [rows_of(row) for row in range(X_ROWS, CHUNK)]
        projs.append([pieces[0], pieces[1], pieces[2][0:16]])
        low = pieces[3][16:32]
        even_16 = even[0:16]
        vec = jnp.concatenate(
            [
                pieces[2][16:32] + jnp.where(even_16, low, 0.0),
                pieces[3][0:16] + jnp.where(even_16, roll(low, -1, 1), 0.0),
            ],
            axis=0,
        )
        vecs.append(vec)
        taps = jnp.where(even[0:16], vec[0:16], roll(vec[0:16], 1, 1))
        total = jnp.zeros((slabs, LANES), F32) + taps[9:10, :]
        for side in range(3):
            above, below = taps[side : side + 1, :], taps[6 + side : 7 + side, :]
            beyond = jnp.where(even, swapped_of(side, -1), swapped_of(side, 1))
            total = total + jnp.where(even[0:1], above, below) * beyond
            total = total + jnp.where(even[0:1], below, above) * swapped_of(side, 0)
            total = total + taps[3 + side : 4 + side, :] * rows_of(side)
        conv.append(silu(total).astype(BF16).astype(F32))

    shared = scr[CHUNK - 1, pl.ds(lax.axis_index("ch") ^ 2, slabs, stride=4), :]
    for way, value in enumerate(
        (jnp.where(even, shared, roll(shared, 1, 1)), jnp.where(even, roll(shared, -1, 1), shared))
    ):
        near_ref[16 * way : 16 * way + 16, :] = value[0:16] * NEG_LOG2E
        near_ref[32 + 8 * way : 40 + 8 * way, :] = value[16:24]
        near_ref[48 + way : 49 + way, :] = value[24:25]
        if way == 0:
            near_ref[52:53, :] = value[25:26]
    near_ref[50:52, :] = jnp.zeros((2, LANES), F32)
    near_ref[53:56, :] = jnp.zeros((3, LANES), F32)

    chans = dtw_ref.shape[2]
    dup = spread(chans, 0) + spread(chans, 1)
    row_weights(dtw_ref, dtb_ref, rate_ref, skip_ref, own_ref, dup)
    steps_ref[...] = step_weights((own_ref, near_ref))

    def from_even(left, right):
        mask = iota(left.shape, 1) % 2 == 0
        return jnp.where(mask, left, roll(right, 1, 1))

    def from_odd(left, right):
        mask = iota(left.shape, 1) % 2 == 0
        return jnp.where(mask, roll(left, -1, 1), right)

    def all_groups(take, parts):
        return jnp.concatenate([take(parts[0], parts[1]), take(parts[2], parts[3])], axis=1)

    values = jnp.concatenate([all_groups(from_even, conv), all_groups(from_odd, conv)], axis=0)
    values_b = values.astype(BF16)
    proj_w = jnp.concatenate(
        [
            all_groups(take, [p[piece] for p in projs])
            for take in (from_even, from_odd)
            for piece in range(3)
        ],
        axis=0,
    ).astype(BF16)
    vec = jnp.concatenate([all_groups(from_even, vecs), all_groups(from_odd, vecs)], axis=0)

    nt = (((1,), (1,)), ((), ()))
    proj = lax.dot_general(values_b, proj_w[0:128], nt, preferred_element_type=F32)
    proj = proj.astype(BF16)
    low = proj[:, 0:16]
    proj = proj.astype(F32)
    turned = lax.dot_general(proj_w[96:160], values_b, nt, preferred_element_type=F32)
    turned = turned.astype(BF16)

    dt_rows = vec[16:32]
    second_half = iota((16, 256), 0) >= 8
    rates = []
    for way in range(2):
        chosen = jnp.where(second_half == (way == 1), dt_rows, 0.0)
        delta = softplus(two_part_dot(low, *halves(chosen)) + vec[10 + way : 11 + way, :])
        drive = delta * values
        scaled = vec[32 + 16 * way : 48 + 16 * way] * NEG_LOG2E
        rates.append([scaled[:, 0:LANES], scaled[:, LANES:]])
        for block in range(2):
            lanes = slice(LANES * block, LANES * block + LANES)
            delta_scr[way, block] = delta[:, lanes]
            drive_scr[way, block] = drive[:, lanes]

    def row_of(at):
        return (at % 2) * slabs + at // 2

    ones = jnp.ones((64, LANES), BF16)

    def expand(way, first):
        tops = (32 * way, 32 * way + 16)
        return lane_rows([turned[top : top + 16] for top in tops], [row_of(first + j) for j in range(8)], mask_ref, ones)

    scan_pair(2 * slabs, rates, delta_scr, drive_scr, expand, wide_scr, part_scr, row_of)

    skip = vec[12:13] + vec[13:14]
    backs = []
    for block in range(2):
        lanes = slice(LANES * block, LANES * block + LANES)
        y = outputs_of(part_scr, block, half_scr) + skip[:, lanes] * values[:, lanes]
        y_even, y_odd = y[0:slabs], y[slabs:]
        backs.append(jnp.where(even, y_even, roll(y_odd, 1, 1)))
        backs.append(jnp.where(even, roll(y_even, -1, 1), y_odd))
    for group in range(4):
        near = group ^ 2
        parts = (backs[group], conv[group], proj[0:slabs], proj[slabs:], backs[near], conv[near])
        for row, value in enumerate(parts):
            scr[row, pl.ds(group, slabs, stride=4), :] = value
    for row in range(BACK):
        back_scr[pl.ds(row, LANES, stride=BACK), :] = scr[row, 0:LANES, :]
    send_ref[...] = back_scr[...].astype(BF16)


def row_kernel(
    recv_ref,
    mask_ref,
    own_ref,
    near_ref,
    steps_ref,
    comb_ref,
    sums_ref,
    scr,
    mixed_scr,
    delta_scr,
    drive_scr,
    part_scr,
    half_scr,
    wide_scr,
):
    cols = LANES
    scr[...] = recv_ref[...].astype(F32)

    def chunk_row(row):
        return scr[pl.ds(row, cols, stride=BACK), :]

    proj = [chunk_row(2), chunk_row(3)]
    lane = iota((cols, LANES), 1)
    both = jnp.where(lane < 32, proj[0], roll(proj[1], 32, 1))
    both = both[:, 0:64].astype(BF16)
    low_rank = two_part_dot(both, steps_ref[0:64, :], steps_ref[64:, :])
    vecs = (own_ref, near_ref)
    verticals = (chunk_row(0), chunk_row(4))
    values = (chunk_row(1), chunk_row(5))
    for block in range(2):
        for way in range(2):
            first = LANES * (2 * block + way)
            delta = softplus(
                low_rank[:, first : first + LANES] + vecs[block][48 + way : 49 + way, :]
            )
            delta_scr[way, block] = delta
            drive_scr[way, block] = delta * values[block]
    rates = [[vec[16 * way : 16 * way + 16, :] for vec in vecs] for way in range(2)]

    for row in range(2):
        mixed_scr[pl.ds(row, cols, stride=2), :] = proj[row]
    turned = mixed_scr[...].T
    alike = iota((LANES, LANES), 0) % 2 == iota((LANES, LANES), 1) % 2
    by_row = jnp.where(alike, 1.0, 0.0).astype(BF16)

    def expand(way, first):
        start = LANES * (first // 64)
        tops = (32 + 32 * way, 48 + 32 * way)
        parts = [turned[top : top + 16, start : start + LANES].astype(BF16) for top in tops]
        return lane_rows(parts, [(first + j) % 64 for j in range(8)], mask_ref, by_row)

    scan_pair(cols, rates, delta_scr, drive_scr, expand, wide_scr, part_scr, lambda at: at)
    sums = [jnp.zeros((8, LANES), F32) for _ in range(2)]
    for block in range(2):
        combined = (
            outputs_of(part_scr, block, half_scr)
            + vecs[block][52:53, :] * values[block]
            + verticals[block]
        )
        combined = combined.T
        if block == 0:
            comb_ref[...] = combined
        for tile in range(LANES // 8):
            rows = combined[8 * tile : 8 * tile + 8]
            sums = [sums[0] + rows, sums[1] + rows * rows]
    for index, value in enumerate(sums):
        value = value + roll(value, 4, 0)
        value = value + roll(value, 2, 0)
        sums_ref[8 * index : 8 * index + 8, :] = value


def gate_kernel(sums_ref, gain_ref, bias_ref, gate_in_ref, affine_ref):
    chans = gain_ref.shape[1]
    gate = silu(gate_in_ref[...].astype(F32))
    pick = iota((LANES, chans), 0) // 2 == iota((LANES, chans), 1)
    for index, ref in enumerate((gain_ref, bias_ref)):
        column = jnp.sum(jnp.where(pick, ref[...], 0.0), axis=1, keepdims=True)
        affine_ref[index] = column * gate


def norm_kernel(total_chans, comb_ref, s0_ref, s1_ref, affine_ref, out_ref):
    sums = s0_ref[...] + s1_ref[...]
    mean = sums[0:8] / total_chans
    var = sums[8:16] / total_chans - mean * mean
    scale = lax.rsqrt(var + 1e-05)
    comb = comb_ref[...]
    means = jnp.concatenate([mean] * (LANES // 8), axis=0)
    scales = jnp.concatenate([scale] * (LANES // 8), axis=0)
    out_ref[...] = ((comb - means) * scales * affine_ref[0] + affine_ref[1]).astype(BF16)


VMEM = pl.BlockSpec(memory_space=pltpu.VMEM)


def call(kernel, name, outs, scratch, inputs, place=VMEM, grant=24 << 20):
    single = not isinstance(outs, (list, tuple))
    return pl.pallas_call(
        kernel,
        out_shape=outs,
        in_specs=[place] * len(inputs),
        out_specs=VMEM if single else [VMEM] * len(outs),
        scratch_shapes=scratch,
        name=name,
        compiler_params=pltpu.CompilerParams(vmem_limit_bytes=grant),
    )(*inputs)


def other(value, flip):
    return lax.ppermute(value, "ch", [(i, i ^ flip) for i in range(lax.axis_size("ch"))])


def exchange(value, chunk, tile):
    peers = value.shape[0] // chunk
    pieces = value.reshape(peers, chunk // tile, tile, LANES)
    moved = lax.all_to_all(pieces, ("sp", "ch"), split_axis=0, concat_axis=0, tiled=True)
    return moved.reshape(value.shape)


def on_device(
    x_in,
    gate_in,
    conv_weight,
    conv_bias,
    proj_weight,
    dt_weight,
    dt_bias,
    decay_rate,
    skip_gain,
    norm_gain,
    norm_bias,
):
    chans, rows, cols = x_in.shape
    total_chans = chans * lax.axis_size("ch")
    flat = (chans * rows, cols)
    struct = jax.ShapeDtypeStruct

    def vm(*shape):
        return pltpu.VMEM(shape, F32)

    dt_weight = dt_weight.transpose(0, 2, 1)
    decay_rate = decay_rate.transpose(0, 2, 1)
    arguments = [
        pltpu.with_memory_space_constraint(value, pltpu.HBM)
        for value in (
            x_in.reshape(flat),
            conv_weight.T,
            conv_bias.reshape(1, chans),
            proj_weight,
            dt_weight,
            dt_bias,
            decay_rate,
            skip_gain,
            norm_gain.reshape(1, chans),
            norm_bias.reshape(1, chans),
            gate_in.reshape(flat),
        )
    ]
    send, col_mask, row_mask, *handed = call(
        prep_kernel,
        "prep",
        [
            struct((CHUNK * cols, LANES), BF16),
            struct((64 * 16, 64), BF16),
            struct((64 * 16, LANES), BF16),
        ]
        + [struct(value.shape, value.dtype) for value in arguments[4:]],
        [
            vm(CHUNK * (cols + 4), LANES),
            vm(CHUNK, LANES),
            vm(2 * VEC_PAIRS, chans),
            vm(64, chans),
            vm(160, LANES),
        ]
        + [pltpu.VMEM(value.shape, value.dtype) for value in arguments[:4]]
        + [pltpu.SemaphoreType.DMA((len(arguments),))],
        arguments,
        pl.BlockSpec(memory_space=pltpu.HBM),
    )
    send, own, near, steps = call(
        column_kernel,
        "columns",
        [
            struct((BACK * cols, LANES), BF16),
            struct((56, LANES), F32),
            struct((56, LANES), F32),
            struct((LANES, 4 * LANES), BF16),
        ],
        [
            vm(CHUNK * cols, LANES),
            vm(BACK * cols, LANES),
            vm(CHUNK, cols, LANES),
            vm(X_ROWS, cols + 16, LANES),
            vm(2, 2, 64, LANES),
            vm(2, 2, 64, LANES),
            vm(2, 2, 8 * 64, LANES),
            vm(LANES, LANES),
            vm(2, 2, 16 * 64, LANES),
        ],
        [exchange(send, CHUNK, CHUNK), col_mask] + handed[:4],
    )
    received = exchange(send, BACK, 2)
    combined, sums = call(
        row_kernel,
        "rows",
        [struct((LANES, cols), F32), struct((16, cols), F32)],
        [
            vm(BACK * cols, LANES),
            vm(2 * cols, LANES),
            vm(2, 2, cols, LANES),
            vm(2, 2, cols, LANES),
            vm(2, 2, 8 * cols, LANES),
            vm(2 * cols, LANES),
            vm(2, 2, 16 * cols, LANES),
        ],
        [received, row_mask, own, near, steps],
    )
    affine = call(
        gate_kernel, "gate", struct((2, LANES, cols), F32), [], [sums] + handed[4:]
    )
    out = call(
        lambda *refs: norm_kernel(total_chans, *refs),
        "norm",
        struct(flat, BF16),
        [],
        [combined, sums, other(sums, 1), affine],
    )
    return out.reshape(chans, rows, cols)


def solution(mesh):
    placed = (
        P("ch", "sp", None),
        P("ch", "sp", None),
        P("ch", None),
        P("ch"),
        P(None, None, "ch"),
        P(None, "ch", None),
        P(None, "ch"),
        P(None, "ch", None),
        P(None, "ch"),
        P("ch"),
        P("ch"),
    )
    return jax.shard_map(
        on_device, mesh=mesh, in_specs=placed, out_specs=P("ch", "sp", None), check_vma=False
    )
```
